256 devices in a mesh: dp: 16 (over z, x_hi), seq: 4 (over y), tensor: 4 (over x_lo, core).
Axes of the slice: x: 4 (x_hi: 2, x_lo: 2; x = x_hi * 2 + x_lo), y: 4, z: 8, core: 2. Of those that a mesh axis runs over, the one named last changes fastest.
Arguments:
- attention_output_rows: bfloat16 [16, 4096, 4096], P('dp', 'seq', 'tensor'), may hold values from -6 to 6
- projection_result_gradient: bfloat16 [16, 4096, 4096], P('dp', 'seq'), may hold values from -6 to 6
- adapter_down_weight: bfloat16 [4096, 128], P('tensor'), may hold values from -0.09375 to 0.09375
- adapter_up_weight: bfloat16 [128, 4096], P(None, 'tensor'), may hold values from -0.09375 to 0.09375
- output_projection_weight: bfloat16 [4096, 4096], P('tensor'), may hold values from -0.09375 to 0.09375
- adam_first_moments: float32 [2, 128, 4096], P(None, 'dp', 'tensor'), may hold values from -24 to 24
- adam_second_moments: float32 [2, 128, 4096], P(None, 'dp', 'tensor'), may hold values from 1 to 40
- rank_side_projection: float32 [16, 128], replicated, may hold values from -0.5 to 0.5
- width_side_projection: bfloat16 [4096, 256], replicated, may hold values from -0.09375 to 0.09375
- bounds: int32 [16, 2, 16], P('dp'), may hold values from 0 to 4096, as said below
- example_owner_slot: int32 [16, 16], P('dp'), may hold values from 0 to 15, each once within a row
Outputs:
- attention_out_gradient: bfloat16 [16, 4096, 4096], P('dp', 'seq', 'tensor')
- features: float32 [16, 16, 8192], P('dp', ('seq', 'tensor'))
The draws below stay inside these ranges and needn't reach their ends.
Inputs may be any that keep to these rules, and one draw needn't show every extreme that they name: bounds[s, 0, e] is the first token of example e of pack s and bounds[s, 1, e] its end (exclusive): the first start is 0, each end is the next start, the last end is 4096, every example has one token or more. The tokens of one aligned block of 1024 tokens of a pack belong to at most 8 examples, and every pack has a block whose tokens belong to exactly 8. `example_owner_slot`: each row names every slot once.
All inputs are finite; a program needn't handle non-finite values.
Results may differ from the reference program's by a relative error of at most 0.014.
Values may be sent and summed in bfloat16 or wider, within the bound.
A program may use at most 128 MiB of HBM per device.

```python
import math
import jax
import jax.numpy as jnp
from jax import lax

MODEL_WIDTH = 4096
ADAPTER_RANK = 128
LEN = 4096
EX = 16
TOUCH = 8
KR = 16
KD = 256
BLK = 1024
SEQS = 16
GROUPS = 16
SLOTS = 16
PROJ = 8192
N_SEQ = 4


def pack_bounds(key):
    n_blocks = LEN // BLK
    others = n_blocks - 2
    remaining = EX - TOUCH
    key_empty, key_full, key_share, key_place = jax.random.split(key, 4)
    empty_block = jax.random.randint(key_empty, (), 1, n_blocks - 1)
    full_pick = jax.random.randint(key_full, (), 0, n_blocks - 1)
    full_block = full_pick + (full_pick >= empty_block).astype(jnp.int32)
    shuffled = jax.random.permutation(key_share, others)
    other_counts = remaining // others + (shuffled < remaining % others).astype(jnp.int32)
    blocks = jnp.arange(n_blocks, dtype=jnp.int32)
    ranked = blocks - (blocks > empty_block).astype(jnp.int32) - (blocks > full_block).astype(jnp.int32)
    ranked = jnp.clip(ranked, 0, others - 1)
    counts = jnp.where(blocks == full_block, TOUCH - 1, jnp.where(blocks == empty_block, 0, other_counts[ranked]))

    def block_cuts(block):
        picked = jax.random.permutation(jax.random.fold_in(key_place, block), BLK - 1)[:TOUCH - 1] + 1
        kept_mask = jnp.arange(TOUCH - 1) < counts[block]
        return jnp.where(kept_mask, block * BLK + picked, LEN)
    cut_points = jnp.sort(jax.vmap(block_cuts)(blocks).reshape(-1))[:EX - 1]
    anchor = jnp.zeros((1,), jnp.int32)
    finish = jnp.full((1,), LEN, jnp.int32)
    starts = jnp.concatenate([anchor, cut_points.astype(jnp.int32)])
    end_points = jnp.concatenate([cut_points.astype(jnp.int32), finish])
    return jnp.stack([starts, end_points]).astype(jnp.int32)


def draw_bounds(key, part):
    sub_keys = jax.random.split(key, SEQS)
    return jax.vmap(pack_bounds)(sub_keys)


def shard_levels(key, shape, cuts, least, top_value):
    def one(position, blocks):
        heights = jax.random.uniform(jax.random.fold_in(jax.random.fold_in(key, 6), position), (blocks,), jnp.float32, least / len(cuts), top_value / len(cuts))
        return jnp.repeat(jnp.exp(heights), shape[position] // blocks).reshape((-1,) + (1,) * (len(shape) - position - 1))

    gain = one(*cuts[0])
    for cut in cuts[1:]:
        gain = gain * one(*cut)
    return gain


def gaussian(stream_key, dims, spread, limit, cuts=(), kind=jnp.bfloat16):
    drawn = spread * jax.random.normal(stream_key, dims, jnp.float32)
    if cuts:
        drawn = drawn * shard_levels(stream_key, dims, cuts, -0.22, 0.18)
    return jnp.clip(drawn, -limit, limit).astype(kind)


def setup_inputs(seed: int = 0) -> dict:
    streams_of = jax.random.split(jax.random.key(seed), 12)
    attention_output_rows = gaussian(streams_of[0], (SEQS, LEN, MODEL_WIDTH), 1.0, 6.0, ((0, 16), (1, 4), (2, 4)))
    projection_result_gradient = gaussian(streams_of[1], (SEQS, LEN, MODEL_WIDTH), 1.0, 6.0, ((0, 16), (1, 4)))
    adapter_down_weight = gaussian(streams_of[2], (MODEL_WIDTH, ADAPTER_RANK), MODEL_WIDTH ** -0.5, 0.09375, ((0, 4),))
    adapter_up_weight = gaussian(streams_of[3], (ADAPTER_RANK, MODEL_WIDTH), MODEL_WIDTH ** -0.5, 0.09375, ((1, 4),))
    output_projection_weight = gaussian(streams_of[4], (MODEL_WIDTH, MODEL_WIDTH), MODEL_WIDTH ** -0.5, 0.09375, ((0, 4),))
    adam_first_moments = gaussian(streams_of[5], (2, ADAPTER_RANK, MODEL_WIDTH), 4.0, 24.0, ((1, 16), (2, 4)), jnp.float32)
    adam_second_moments = jnp.clip(jnp.exp(math.log(40.0) - 3.6888795 * jax.random.uniform(streams_of[6], (2, ADAPTER_RANK, MODEL_WIDTH), jnp.float32) ** shard_levels(streams_of[6], (2, ADAPTER_RANK, MODEL_WIDTH), ((1, 16), (2, 4)), -0.2, 0.2)), 1.0, 40.0)
    rank_side_projection = gaussian(streams_of[7], (KR, ADAPTER_RANK), ADAPTER_RANK ** -0.5, 0.5, (), jnp.float32)
    width_side_projection = gaussian(streams_of[8], (MODEL_WIDTH, KD), MODEL_WIDTH ** -0.5, 0.09375)
    bounds = draw_bounds(jax.random.fold_in(streams_of[11], 71), 0)
    example_owner_slot = jax.vmap(lambda own: jax.random.permutation(own, SLOTS))(jax.random.split(streams_of[10], GROUPS)).reshape((GROUPS, SLOTS)).astype(jnp.int32)
    return {"attention_output_rows": attention_output_rows, "projection_result_gradient": projection_result_gradient, "adapter_down_weight": adapter_down_weight, "adapter_up_weight": adapter_up_weight, "output_projection_weight": output_projection_weight, "adam_first_moments": adam_first_moments, "adam_second_moments": adam_second_moments, "rank_side_projection": rank_side_projection, "width_side_projection": width_side_projection, "bounds": bounds, "example_owner_slot": example_owner_slot}


ADAPTER_SCALE = 4.0
BETA_ONE = 0.9
BETA_TWO = 0.999
EPSILON = 1e-08

def contract_trailing(left, right):
    return lax.dot_general(left, right, (((1,), (1,)), ((), ())), preferred_element_type=jnp.float32)

def normalize(grads, adam_first_moments, adam_second_moments):
    first = BETA_ONE * adam_first_moments + (1.0 - BETA_ONE) * grads
    second = BETA_TWO * adam_second_moments + (1.0 - BETA_TWO) * grads * grads
    return (first / (jnp.sqrt(second) + EPSILON)).astype(jnp.bfloat16)

def project(normed, rank_side_projection, width_side_projection):
    inner = jnp.einsum('emrd,dc->emrc', normed.astype(jnp.float32), width_side_projection.astype(jnp.float32))
    outer = jnp.einsum('qr,emrc->emqc', rank_side_projection, inner, precision=lax.Precision.HIGHEST)
    return outer.reshape(outer.shape[0], -1)

def bundle_terms(token_count, gradient_result, boundary_row, adapter_down_weight, adapter_up_weight, output_projection_weight, adam_first_moments, adam_second_moments, rank_side_projection, width_side_projection):
    reduced_input = jnp.dot(token_count, adapter_down_weight, preferred_element_type=jnp.float32).astype(jnp.bfloat16)
    reduced_gradient = contract_trailing(gradient_result, adapter_up_weight).astype(jnp.bfloat16)
    attention_out_gradient = (contract_trailing(gradient_result, output_projection_weight) + ADAPTER_SCALE * contract_trailing(reduced_gradient, adapter_down_weight)).astype(jnp.bfloat16)
    positions = jnp.arange(LEN, dtype=jnp.int32)
    example_id = lax.optimization_barrier(jnp.sum((boundary_row[0][None, :] <= positions[:, None]).astype(jnp.int32), axis=1)) - 1
    grads = jnp.zeros((EX, 2, ADAPTER_RANK, MODEL_WIDTH), jnp.float32)
    slot_range = jnp.arange(TOUCH, dtype=jnp.int32)
    for block in range(N_SEQ):
        low_t = block * BLK
        block_ids = example_id[low_t:low_t + BLK]
        first_id = block_ids[0]
        in_slot = ((block_ids - first_id)[:, None] == slot_range[None, :]).astype(jnp.bfloat16)
        masked_grad = (reduced_gradient[low_t:low_t + BLK, None, :] * in_slot[:, :, None]).reshape(BLK, TOUCH * ADAPTER_RANK)
        masked_in = (reduced_input[low_t:low_t + BLK, None, :] * in_slot[:, :, None]).reshape(BLK, TOUCH * ADAPTER_RANK)
        part_a = jnp.einsum('tk,td->kd', masked_grad.astype(jnp.float32), token_count[low_t:low_t + BLK].astype(jnp.float32))
        part_b = jnp.einsum('tk,td->kd', masked_in.astype(jnp.float32), gradient_result[low_t:low_t + BLK].astype(jnp.float32))
        parts = ADAPTER_SCALE * jnp.stack([part_a.reshape(TOUCH, ADAPTER_RANK, MODEL_WIDTH), part_b.reshape(TOUCH, ADAPTER_RANK, MODEL_WIDTH)], axis=1)
        parts = lax.optimization_barrier(parts.astype(jnp.bfloat16)).astype(jnp.float32)
        for slot in range(TOUCH):
            target = jnp.minimum(first_id + slot, EX - 1).astype(jnp.int32)
            grads = grads.at[target].add(parts[slot])
    normed = normalize(grads, adam_first_moments, adam_second_moments)
    return (attention_out_gradient, project(normed, rank_side_projection, width_side_projection))

def reference(attention_output_rows, projection_result_gradient, adapter_down_weight, adapter_up_weight, output_projection_weight, adam_first_moments, adam_second_moments, rank_side_projection, width_side_projection, bounds, example_owner_slot):

    def one_pack(entry_list):
        return bundle_terms(entry_list[0], entry_list[1], entry_list[2], adapter_down_weight, adapter_up_weight, output_projection_weight, adam_first_moments, adam_second_moments, rank_side_projection, width_side_projection)
    attention_out_gradient, feature = lax.map(one_pack, (attention_output_rows, projection_result_gradient, bounds))
    grouped = feature.reshape(GROUPS, SLOTS, PROJ)

    def place(row, values):
        return jnp.zeros((SLOTS, PROJ), jnp.float32).at[row].set(values)
    features = jax.vmap(place)(example_owner_slot, grouped)
    return (attention_out_gradient, features)
```

```python
import functools

import jax
import jax.numpy as jnp
from jax import lax
from jax.experimental import pallas as pl
from jax.experimental.pallas import tpu as pltpu
from jax.sharding import PartitionSpec as P

TOUCH = 8
SCALE = 4.0
BETA_ONE = 0.9
BETA_TWO = 0.999
EPSILON = 1e-08

N_DP, N_SEQ, N_TP = 16, 4, 4
GROUP = N_SEQ * N_TP
BLK = 1024
WIDTH = 4096
COLS = WIDTH // N_TP
RANK = 128
KR, KD = 16, 256
EX = 16
HALF = BLK // 2
TILE = 256
CHUNKS = 4
N_Z = 8

bf16 = jnp.bfloat16
f32 = jnp.float32
NT = (((1,), (1,)), ((), ()))
MESH_ID = pl.DeviceIdType.MESH


def kernel(
    x_hbm, g_hbm, a_hbm, b_hbm, w_hbm, m1_hbm, m2_hbm, r_ref, q_hbm, bounds, owner,
    out_hbm, feat_ref,
    xv, gv, wv, av, bv, qv, m1v, m2v, acc, outv,
    ex1s, ex1r, lowh, ex2s, ex2r, low, low_t, lhs, parts, cs, cr, mom, uv, fv, fsend, frecv,
    ld_sem, out_sem, ex_ss, ex_rs, mx_s, mx_r, mz_s, mz_r, c_ss, c_rs, f_ss, f_rs,
):
    dp = lax.axis_index("dp")
    s = lax.axis_index("seq")
    t = lax.axis_index("tensor")
    core = lax.rem(t, 2)
    chip = lax.div(t, 2)
    partner = chip * 2 + (1 - core)
    across = (1 - chip) * 2 + core
    zi = lax.div(dp, 2)
    xh = lax.rem(dp, 2)
    xpeer = zi * 2 + (1 - xh)
    zright = lax.rem(zi + 1, N_Z)
    zleft = lax.rem(zi + N_Z - 1, N_Z)
    me = s * N_TP + t

    barrier = pltpu.get_barrier_semaphore()

    def greet(j, _):
        o = lax.rem(me + j, GROUP)
        pl.semaphore_signal(
            barrier, inc=1, device_id={"seq": lax.div(o, N_TP), "tensor": lax.rem(o, N_TP)},
            device_id_type=MESH_ID)
        return 0

    lax.fori_loop(1, GROUP, greet, 0)
    for peer in (xpeer, zright * 2 + xh, zleft * 2 + xh):
        pl.semaphore_signal(barrier, inc=1, device_id={"dp": peer}, device_id_type=MESH_ID)

    def col(i):
        return pl.ds(pl.multiple_of(lax.rem(t + i, N_TP) * COLS, COLS), COLS)

    def load(i, src, dst):
        return pltpu.make_async_copy(src, dst, ld_sem.at[i])

    ld_a = load(0, a_hbm, av)
    ld_b = load(1, b_hbm, bv)
    ld_x = load(2, x_hbm, xv)
    ld_g = [load(3 + i, g_hbm.at[:, col(i)], gv.at[:, col(i)]) for i in range(N_TP)]
    ld_m1 = load(7, m1_hbm, m1v)
    ld_m2 = load(8, m2_hbm, m2v)
    ld_q = load(9, q_hbm.at[col(0), :], qv)
    ld_w = [
        load(10 + i, w_hbm.at[pl.ds(i * TILE, TILE), :], wv.at[pl.ds(i * TILE, TILE), :])
        for i in range(4)
    ]
    for c in (ld_a, ld_b, ld_x, ld_g[0], ld_m1, ld_m2, *ld_g[1:], *ld_w, ld_q):
        c.start()

    ld_a.wait()
    ld_b.wait()
    ld_x.wait()
    ld_g[0].wait()

    def partial(h):
        rows = pl.ds(pl.multiple_of(h * HALF, HALF), HALF)
        p_in = jnp.dot(xv[rows, :], av[...], preferred_element_type=f32)
        p_gr = lax.dot_general(gv[rows, col(0)], bv[...], NT, preferred_element_type=f32)
        return p_gr, p_in

    p_gr, p_in = partial(1 - core)
    ex1s[:, :RANK] = p_gr.astype(bf16)
    ex1s[:, RANK:] = p_in.astype(bf16)

    pl.semaphore_wait(barrier, GROUP - 1 + 3)

    def rcopy(src, dst, ss, rs, **where):
        return pltpu.make_async_remote_copy(
            src_ref=src, dst_ref=dst, send_sem=ss, recv_sem=rs, device_id=where,
            device_id_type=MESH_ID)

    ex1 = rcopy(ex1s, ex1r, ex_ss.at[0], ex_rs.at[0], tensor=partner)
    ex1.start()

    ld_m1.wait()
    ld_m2.wait()
    for m in range(2):
        mom[zi, xh, m] = jnp.concatenate([m1v[m], m2v[m]], axis=0).astype(bf16)
    mx = rcopy(mom.at[zi, xh], mom.at[zi, xh], mx_s, mx_r, dp=xpeer)
    mx.start()
    mx_in = rcopy(mom.at[zi, xh], mom.at[zi, 1 - xh], mx_s, mx_r, dp=xpeer)

    p_gr, p_in = partial(core)
    lowh[:, :RANK] = p_gr
    lowh[:, RANK:] = p_in

    right_dp = zright * 2 + xh
    left_dp = zleft * 2 + xh

    def ring(j):
        zr = lax.rem(zi + N_Z - j, N_Z)
        zl = lax.rem(zi + j, N_Z)
        if j < 3:
            a = mom.at[zr]
            b = mom.at[zl]
        else:
            a = mom.at[zr, 0]
            b = mom.at[zl, 1]
        return (
            rcopy(a, a, mz_s.at[j, 0], mz_r.at[j, 0], dp=right_dp),
            rcopy(b, b, mz_s.at[j, 1], mz_r.at[j, 1], dp=left_dp),
        )

    def ring_in(j):
        zr = lax.rem(zi + N_Z - j - 1, N_Z)
        zl = lax.rem(zi + j + 1, N_Z)
        if j < 3:
            a = mom.at[zr]
            b = mom.at[zl]
        else:
            a = mom.at[zr, 0]
            b = mom.at[zl, 1]
        return (
            rcopy(a, a, mz_s.at[j, 0], mz_r.at[j, 0], dp=right_dp),
            rcopy(b, b, mz_s.at[j, 1], mz_r.at[j, 1], dp=left_dp),
        )

    def ring_start(j):
        for c in ring(j):
            c.start()

    def ring_wait(j):
        for c in ring_in(j):
            c.wait_recv()

    def main_tile(n):
        acc[:, n * TILE:(n + 1) * TILE] = lax.dot_general(
            gv[...], wv[n * TILE:(n + 1) * TILE, :], NT, preferred_element_type=f32)

    for c in ld_g[1:]:
        c.wait()
    ld_w[0].wait()
    main_tile(0)

    ex1.wait_recv()
    total = lowh[...] + ex1r[...].astype(f32)
    lowh[...] = total
    ex2s[...] = total.astype(bf16)
    ex2 = rcopy(ex2s, ex2r, ex_ss.at[1], ex_rs.at[1], tensor=across)
    ex2.start()

    mx_in.wait_recv()
    ring_start(0)
    ld_w[1].wait()
    main_tile(1)
    ld_w[2].wait()
    main_tile(2)
    ring_wait(0)
    ring_start(1)
    ld_w[3].wait()
    main_tile(3)

    ex2.wait_recv()
    low[core] = (lowh[...] + ex2r[...].astype(f32)).astype(bf16)
    ex3 = rcopy(low.at[core], low.at[core], ex_ss.at[2], ex_rs.at[2], tensor=partner)
    ex3_in = rcopy(low.at[1 - core], low.at[1 - core], ex_ss.at[2], ex_rs.at[2], tensor=partner)
    ex3.start()

    low_pos = s * BLK
    n_le = jnp.int32(0)
    n_lt = jnp.int32(0)
    n_last = jnp.int32(0)
    pos = low_pos + lax.broadcasted_iota(jnp.int32, (1, BLK), 1)
    slot = jnp.zeros((1, BLK), jnp.int32)
    for e in range(EX):
        st = bounds[0, e]
        n_le = n_le + (st <= low_pos).astype(jnp.int32)
        n_lt = n_lt + (st < low_pos).astype(jnp.int32)
        n_last = n_last + (st <= low_pos + BLK - 1).astype(jnp.int32)
        slot = slot + (st <= pos).astype(jnp.int32)
    first_id = n_le - 1
    last_id = n_last - 1
    slot = slot - n_le
    n_slots = last_id - first_id
    continued = (n_le == n_lt).astype(f32)
    keep = continued * (first_id == last_id).astype(f32)

    ex3_in.wait_recv()
    for h in range(2):
        low_t[:, h * HALF:(h + 1) * HALF] = (low[h].astype(f32) * SCALE).T.astype(bf16)

    m_last = (slot == n_slots).astype(f32).astype(bf16)
    for m in range(2):
        left = low_t[m * RANK:(m + 1) * RANK, :] * m_last
        right = xv[...] if m == 0 else gv[:, col(0)]
        p = jnp.dot(left, right, preferred_element_type=f32).astype(bf16)
        cs[2 * m] = p[:64]
        cs[2 * m + 1] = p[64:]

    @pl.when(s == 0)
    def _():
        cr[...] = jnp.zeros_like(cr)

    nxt = lax.rem(s + 1, N_SEQ)

    def chain_copy(c):
        return rcopy(cs.at[c], cr.at[c], c_ss.at[c], c_rs.at[c], seq=nxt)

    def chain(p):
        c = p - s

        @pl.when((c >= 0) & (c < CHUNKS) & (s < N_SEQ - 1))
        def _():
            @pl.when(s > 0)
            def _():
                chain_copy(c).wait_recv()
                cs[c] = (cs[c].astype(f32) + keep * cr[c].astype(f32)).astype(bf16)

            chain_copy(c).start()

    chain(0)

    def build(m):
        def one(k, _):
            mask = (slot == k).astype(f32).astype(bf16)
            lhs[pl.ds(pl.multiple_of(k * RANK, RANK), RANK), :] = (
                low_t[m * RANK:(m + 1) * RANK, :] * mask)
            return 0

        lax.fori_loop(0, TOUCH, one, 0)

    def part_tiles(m):
        def one(n, _):
            c0 = pl.ds(pl.multiple_of(n * TILE, TILE), TILE)
            if m == 0:
                right = xv[:, c0]
            else:
                right = gv[:, pl.ds(pl.multiple_of(t * COLS + n * TILE, TILE), TILE)]
            parts[m, :, c0] = jnp.dot(lhs[...], right, preferred_element_type=f32).astype(bf16)
            return 0

        lax.fori_loop(0, COLS // TILE, one, 0)

    ring_wait(1)
    ring_start(2)
    build(0)
    part_tiles(0)
    chain(1)
    build(1)
    part_tiles(1)
    chain(2)
    ring_wait(2)
    ring_start(3)

    def fix(i, _):
        rows = pl.ds(pl.multiple_of(i * TILE, TILE), TILE)
        h = lax.div(i, 2)
        sub = pl.ds(pl.multiple_of(lax.rem(i, 2) * TILE, TILE), TILE)
        lg = low[h, sub, :RANK]
        corr = lax.dot_general(lg, av[...], NT, preferred_element_type=f32)
        outv[rows, :] = (acc[rows, :] + SCALE * corr).astype(bf16)
        return 0

    lax.fori_loop(0, BLK // TILE, fix, 0)
    out_copy = pltpu.make_async_copy(outv, out_hbm, out_sem)
    out_copy.start()
    chain(3)

    r = r_ref[...]
    r_hi = r.astype(bf16)
    r_lo = (r - r_hi.astype(f32)).astype(bf16)
    r2 = jnp.concatenate([r_hi, r_lo], axis=0)

    def normalized(k, m, incoming):
        for c in range(COLS // TILE):
            cc = slice(c * TILE, (c + 1) * TILE)
            rows = []
            for d in range(0, N_DP, 2):
                a = mom[d // 2, 0, m, :, cc].astype(f32)
                b = mom[d // 2, 1, m, :, cc].astype(f32)
                m1 = jnp.concatenate([a[:8], b[:8]], axis=0)
                m2 = jnp.concatenate([a[8:], b[8:]], axis=0)
                g = parts[m, pl.ds(pl.multiple_of(k * RANK + d * 8, 16), 16), cc].astype(f32)
                if incoming:
                    ch = 2 * m + d // 8
                    g = g + continued * cr[ch, (d % 8) * 8:(d % 8) * 8 + 16, cc].astype(f32)
                first = BETA_ONE * m1 + (1.0 - BETA_ONE) * g
                second = BETA_TWO * m2 + (1.0 - BETA_TWO) * (g * g)
                root = second * lax.rsqrt(second) + EPSILON
                rows.append((first * lax.rsqrt(root * root)).astype(bf16))
            n = jnp.concatenate(rows, axis=0)
            u = jnp.dot(r2, n, preferred_element_type=f32)
            u = u[:KR] + u[KR:]
            hi = u.astype(bf16)
            uv[k, m, 0, :, cc] = hi
            uv[k, m, 1, :, cc] = (u - hi.astype(f32)).astype(bf16)

    def slots(lo, hi):
        def one(i, _):
            normalized(lax.div(i, 2), lax.rem(i, 2), False)
            return 0

        lax.fori_loop(2 * lo, 2 * hi, one, 0)

    ring_wait(3)
    ld_q.wait()
    slots(1, 3)
    chain(4)
    slots(3, 6)
    chain(5)
    slots(6, 8)

    @pl.when(s == N_SEQ - 1)
    def _():
        for c in range(CHUNKS):
            chain_copy(c).wait_recv()

    for m in range(2):
        normalized(0, m, True)

    def widths(k, _):
        u = uv[k].reshape(2 * 2 * KR, COLS)
        f = jnp.dot(u, qv[...], preferred_element_type=f32)
        fv[k, :KR] = f[:KR] + f[KR:2 * KR]
        fv[k, KR:] = f[2 * KR:3 * KR] + f[3 * KR:]
        return 0

    lax.fori_loop(0, TOUCH, widths, 0)

    goes = []
    for k in range(TOUCH):
        e = jnp.minimum(first_id + k, EX - 1)
        done = (k <= n_slots) & (bounds[1, e] <= low_pos + BLK)
        goes.append(jnp.where(done, owner[0, e], -1))

    def place(o, _):
        total = jnp.zeros((2 * KR, KD), f32)
        for k in range(TOUCH):
            total = total + jnp.where(goes[k] == o, 1.0, 0.0) * fv[k]
        fsend[o] = total.astype(bf16)
        return 0

    lax.fori_loop(0, GROUP, place, 0)

    def feature_copy(o, j):
        return rcopy(
            fsend.at[o], frecv.at[me], f_ss.at[j], f_rs.at[me],
            seq=lax.div(o, N_TP), tensor=lax.rem(o, N_TP))

    def send_out(j, _):
        feature_copy(lax.rem(me + j, GROUP), j).start()
        return 0

    lax.fori_loop(1, GROUP, send_out, 0)
    frecv[me] = fsend[me]

    def arrive(j, _):
        o = lax.rem(me + j, GROUP)
        rcopy(fsend.at[o], frecv.at[o], f_ss.at[j], f_rs.at[o],
              seq=lax.div(o, N_TP), tensor=lax.rem(o, N_TP)).wait_recv()
        return 0

    lax.fori_loop(1, GROUP, arrive, 0)
    feat = jnp.zeros((2 * KR, KD), f32)
    for o in range(GROUP):
        feat = feat + frecv[o].astype(f32)
    feat_ref[...] = feat

    ex1.wait_send()
    ex2.wait_send()
    ex3.wait_send()
    mx.wait_send()
    for j in range(4):
        for c in ring(j):
            c.wait_send()

    @pl.when(s < N_SEQ - 1)
    def _():
        for c in range(CHUNKS):
            chain_copy(c).wait_send()

    def left(j, _):
        feature_copy(lax.rem(me + j, GROUP), j).wait_send()
        return 0

    lax.fori_loop(1, GROUP, left, 0)
    out_copy.wait()


def per_device(x, g, a, b, w, m1, m2, r, q, bounds, owner):
    any_ = pl.BlockSpec(memory_space=pl.ANY)
    vmem = pl.BlockSpec(memory_space=pltpu.VMEM)
    smem = pl.BlockSpec(memory_space=pltpu.SMEM)
    dma = pltpu.SemaphoreType.DMA
    V = pltpu.VMEM
    att, feat = pl.pallas_call(
        kernel,
        out_shape=(
            jax.ShapeDtypeStruct((BLK, COLS), bf16),
            jax.ShapeDtypeStruct((2 * KR, KD), f32),
        ),
        in_specs=[any_] * 7 + [vmem, any_, smem, smem],
        out_specs=(any_, vmem),
        scratch_shapes=[
            V((BLK, COLS), bf16), V((BLK, WIDTH), bf16), V((COLS, WIDTH), bf16),
            V((COLS, RANK), bf16), V((RANK, COLS), bf16), V((COLS, KD), bf16),
            V((2, 8, COLS), f32), V((2, 8, COLS), f32),
            V((BLK, COLS), f32), V((BLK, COLS), bf16),
            V((HALF, 2 * RANK), bf16), V((HALF, 2 * RANK), bf16), V((HALF, 2 * RANK), f32),
            V((HALF, 2 * RANK), bf16), V((HALF, 2 * RANK), bf16),
            V((2, HALF, 2 * RANK), bf16), V((2 * RANK, BLK), bf16),
            V((TOUCH * RANK, BLK), bf16), V((2, TOUCH * RANK, COLS), bf16),
            V((CHUNKS, 64, COLS), bf16), V((CHUNKS, 64, COLS), bf16),
            V((N_Z, 2, 2, 16, COLS), bf16),
            V((TOUCH, 2, 2, KR, COLS), bf16), V((TOUCH, 2 * KR, KD), f32),
            V((GROUP, 2 * KR, KD), bf16), V((GROUP, 2 * KR, KD), bf16),
            dma((14,)), dma(()), dma((3,)), dma((3,)), dma(()), dma(()),
            dma((4, 2)), dma((4, 2)), dma((CHUNKS,)), dma((CHUNKS,)),
            dma((GROUP,)), dma((GROUP,)),
        ],
        compiler_params=pltpu.CompilerParams(
            collective_id=0, has_side_effects=True, vmem_limit_bytes=60 * 2**20),
        name="step",
    )(
        x.reshape(BLK, COLS), g.reshape(BLK, WIDTH), a, b, w, m1, m2, r, q,
        bounds.reshape(2, EX), owner.reshape(1, EX),
    )
    return att.reshape(1, BLK, COLS), feat.reshape(1, 1, 2 * KR * KD)


def solution(mesh):
    return jax.shard_map(
        per_device,
        mesh=mesh,
        in_specs=(
            P("dp", "seq", "tensor"),
            P("dp", "seq", None),
            P("tensor", None),
            P(None, "tensor"),
            P("tensor", None),
            P(None, "dp", "tensor"),
            P(None, "dp", "tensor"),
            P(),
            P(),
            P("dp", None, None),
            P("dp", None),
        ),
        out_specs=(P("dp", "seq", "tensor"), P("dp", ("seq", "tensor"), None)),
        check_vma=False,
    )
```

```python
import jax
import jax.numpy as jnp
from jax import lax
from jax.experimental import pallas as pl
from jax.experimental.pallas import tpu as pltpu
from jax.sharding import PartitionSpec as P

TOUCH = 8
SCALE = 4.0
BETA_ONE = 0.9
BETA_TWO = 0.999
EPSILON = 1e-08

N_DP, N_SEQ, N_TP = 16, 4, 4
GROUP = N_SEQ * N_TP
BLK = 1024
WIDTH = 4096
COLS = WIDTH // N_TP
RANK = 128
KR, KD = 16, 256
EX = 16
HALF = BLK // 2
TILE = 256
WIDE = 512
CHUNKS = 4
SIDES = 2
LAG = 2
N_Z = 8
VLIMIT = 60

bf16 = jnp.bfloat16
f32 = jnp.float32
NT = (((1,), (1,)), ((), ()))
MESH_ID = pl.DeviceIdType.MESH


def kernel(
    x_hbm, g_hbm, a_hbm, b_hbm, w_hbm, m1_hbm, m2_hbm, r_hbm, q_hbm, bounds_hbm, owner_hbm,
    out_ref, feat_ref,
    xg, gv, wv, ab, bv, qv, m1v, m2v, rv, bounds, owner, acc,
    ex1s, ex1r, lowh, ex2s, ex2r, low, low_t, parts, cs, cr, mom, uv, facc, fsend, frecv,
    ld_sem, ex_ss, ex_rs, mx_ss, mx_rs, mz_ss, mz_rs, c_ss, c_rs, f_ss, f_rs,
):
    dp = lax.axis_index("dp")
    s = lax.axis_index("seq")
    t = lax.axis_index("tensor")
    core = lax.rem(t, 2)
    chip = lax.div(t, 2)
    partner = chip * 2 + (1 - core)
    across = (1 - chip) * 2 + core
    zi = lax.div(dp, 2)
    xh = lax.rem(dp, 2)
    xpeer = zi * 2 + (1 - xh)
    zright = lax.rem(zi + 1, N_Z)
    zleft = lax.rem(zi + N_Z - 1, N_Z)
    me = s * N_TP + t

    def col(i):
        return pl.ds(pl.multiple_of(lax.rem(t + i, N_TP) * COLS, COLS), COLS)

    def half_rows(h):
        return pl.ds(pl.multiple_of(h * HALF, HALF), HALF)

    def load(i, src, dst):
        return pltpu.make_async_copy(src, dst, ld_sem.at[i])

    ld_b = load(0, b_hbm, bv)
    ld_a = load(1, a_hbm, ab.at[1])
    ld_low = []
    for i, h in enumerate((1 - core, core)):
        ld_low.append(load(2 + 2 * i, g_hbm.at[half_rows(h), col(0)], xg.at[1, half_rows(h), :]))
        ld_low.append(load(3 + 2 * i, x_hbm.at[half_rows(h), :], xg.at[0, half_rows(h), :]))
    ld_m1 = load(6, m1_hbm, m1v)
    ld_m2 = load(7, m2_hbm, m2v)
    ld_g = [load(8 + i, g_hbm.at[:, col(i)], gv.at[:, col(i)]) for i in range(1, N_TP)]
    ld_w = [
        load(12 + i, w_hbm.at[pl.ds(i * WIDE, WIDE), :], wv.at[pl.ds(i * WIDE, WIDE), :])
        for i in range(2)
    ]
    ld_q = load(14, q_hbm.at[col(0), :], qv)
    ld_r = load(15, r_hbm, rv)
    ld_bounds = load(16, bounds_hbm, bounds)
    ld_owner = load(17, owner_hbm, owner)
    own_g = load(8, xg.at[1], gv.at[:, col(0)])
    for c in (ld_b, ld_a, *ld_low, ld_m1, ld_m2, *ld_g, *ld_w, ld_q, ld_r, ld_bounds, ld_owner):
        c.start()

    barrier = pltpu.get_barrier_semaphore()

    def greet(j, _):
        o = lax.rem(me + j, GROUP)
        pl.semaphore_signal(
            barrier, inc=1, device_id={"seq": lax.div(o, N_TP), "tensor": lax.rem(o, N_TP)},
            device_id_type=MESH_ID)
        return 0

    lax.fori_loop(1, GROUP, greet, 0)
    for peer in (xpeer, zright * 2 + xh, zleft * 2 + xh):
        pl.semaphore_signal(barrier, inc=1, device_id={"dp": peer}, device_id_type=MESH_ID)

    def rcopy(src, dst, ss, rs, **where):
        return pltpu.make_async_remote_copy(
            src_ref=src, dst_ref=dst, send_sem=ss, recv_sem=rs, device_id=where,
            device_id_type=MESH_ID)

    ex1 = rcopy(ex1s, ex1r, ex_ss.at[0], ex_rs.at[0], tensor=partner)
    ex2 = rcopy(ex2s, ex2r, ex_ss.at[1], ex_rs.at[1], tensor=across)
    ex3 = rcopy(low.at[core], low.at[core], ex_ss.at[2], ex_rs.at[2], tensor=partner)
    ex3_in = rcopy(low.at[1 - core], low.at[1 - core], ex_ss.at[2], ex_rs.at[2], tensor=partner)

    def mx(m, block):
        return rcopy(mom.at[m, zi, xh], mom.at[m, zi, block], mx_ss.at[m], mx_rs.at[m], dp=xpeer)

    right_dp = zright * 2 + xh
    left_dp = zleft * 2 + xh

    def ring(j, m, ahead):
        zr = lax.rem(zi + N_Z - j - ahead, N_Z)
        zl = lax.rem(zi + j + ahead, N_Z)
        if j < 3:
            a = mom.at[m, zr]
            b = mom.at[m, zl]
        else:
            a = mom.at[m, zr, 0]
            b = mom.at[m, zl, 1]
        return (
            rcopy(a, a, mz_ss.at[j, m, 0], mz_rs.at[j, m, 0], dp=right_dp),
            rcopy(b, b, mz_ss.at[j, m, 1], mz_rs.at[j, m, 1], dp=left_dp),
        )

    def ring_wait(j, m):
        for c in ring(j, m, 1):
            c.wait_recv()

    def ring_step(j, m):
        if j == 0:
            mx(m, 1 - xh).wait_recv()
        else:
            ring_wait(j - 1, m)
        for c in ring(j, m, 0):
            c.start()

    ld_b.wait()
    ab[0] = bv[...].T
    ld_a.wait()

    def partial(i, _):
        m = lax.rem(i, 2)
        late = lax.div(i, 2)
        rows = half_rows(jnp.where(late == 1, core, 1 - core))
        for n in range(4):
            @pl.when(i == n)
            def _():
                ld_low[n].wait()

        p = jnp.dot(xg[1 - m, rows, :], ab[m], preferred_element_type=f32)

        @pl.when(late == 0)
        def _():
            ex1s[m] = p.astype(bf16)

        @pl.when(late == 1)
        def _():
            lowh[m] = p

        @pl.when(i == 1)
        def _():
            pl.semaphore_wait(barrier, GROUP - 1 + 3)
            ex1.start()
            ld_m1.wait()
            ld_m2.wait()
            for mm in range(2):
                mom[mm, zi, xh] = jnp.concatenate([m1v[mm], m2v[mm]], axis=0).astype(bf16)
                mx(mm, xh).start()

        return 0

    lax.fori_loop(0, 4, partial, 0)
    own_g.start()

    for c in ld_g:
        c.wait()
    ld_w[0].wait()
    own_g.wait()

    def main_tile(i, _):
        @pl.when(i == 1)
        def _():
            ex1.wait_recv()
            total = lowh[...] + ex1r[...].astype(f32)
            lowh[...] = total
            ex2s[...] = total.astype(bf16)
            ex2.start()

        @pl.when(i == 2)
        def _():
            ld_w[1].wait()

        @pl.when(i == 3)
        def _():
            ring_step(0, 0)
            ring_step(0, 1)

        rows = half_rows(lax.rem(i, 2))
        cc = pl.ds(pl.multiple_of(lax.div(i, 2) * WIDE, WIDE), WIDE)
        acc[rows, cc] = lax.dot_general(
            gv[rows, :], wv[cc, :], NT, preferred_element_type=f32)
        return 0

    lax.fori_loop(0, 4, main_tile, 0)

    ex2.wait_recv()
    low[core] = (lowh[...] + ex2r[...].astype(f32)).astype(bf16)
    ex3.start()

    ld_bounds.wait()
    ld_owner.wait()
    low_pos = s * BLK
    n_le = jnp.int32(0)
    n_lt = jnp.int32(0)
    n_last = jnp.int32(0)
    n_next = jnp.int32(0)
    pos = low_pos + lax.broadcasted_iota(jnp.int32, (1, BLK), 1)
    ids = jnp.full((1, BLK), -1, jnp.int32)
    for e in range(EX):
        st = bounds[0, e]
        n_le = n_le + (st <= low_pos).astype(jnp.int32)
        n_lt = n_lt + (st < low_pos).astype(jnp.int32)
        n_last = n_last + (st <= low_pos + BLK - 1).astype(jnp.int32)
        n_next = n_next + (st <= low_pos + BLK).astype(jnp.int32)
        ids = ids + (st <= pos).astype(jnp.int32)
    first_id = n_le - 1
    last_id = n_last - 1
    n_slots = last_id - first_id
    single = (first_id == last_id).astype(f32)
    inside = (s < N_SEQ - 1).astype(jnp.int32)
    from_left = (n_le == n_lt).astype(f32)
    from_right = ((n_next == n_last).astype(jnp.int32) * inside).astype(f32)
    begins = (from_left, from_right)
    keeps = (from_left * single, from_right * single)

    def mask_of(side, k):
        slot = jnp.where(side == 0, ids - first_id, last_id - ids)
        return (slot == k).astype(f32).astype(bf16)

    ring_step(1, 0)
    ex3_in.wait_recv()

    def turn(i, _):
        h = lax.div(i, 2)
        m = lax.rem(i, 2)
        rows = pl.ds(pl.multiple_of(m * RANK, RANK), RANK)
        low_t[rows, half_rows(h)] = (low[h, m].astype(f32) * SCALE).T.astype(bf16)
        return 0

    lax.fori_loop(0, 4, turn, 0)

    def rank_rows(m):
        return pl.ds(pl.multiple_of(m * RANK, RANK), RANK)

    def far(i, _):
        m = lax.div(i, 2)
        side = lax.rem(i, 2)
        left = low_t[rank_rows(m), :] * mask_of(side, n_slots)
        p = jnp.dot(left, xg[m, :, half_rows(side)], preferred_element_type=f32).astype(bf16)
        cs[side, 2 * m] = p[:64]
        cs[side, 2 * m + 1] = p[64:]
        return 0

    lax.fori_loop(0, 4, far, 0)

    @pl.when(s == 0)
    def _():
        cr[0] = jnp.zeros((CHUNKS, 64, WIDE), bf16)

    @pl.when(s == N_SEQ - 1)
    def _():
        cr[1] = jnp.zeros((CHUNKS, 64, WIDE), bf16)

    places = (s, N_SEQ - 1 - s)
    nexts = (lax.rem(s + 1, N_SEQ), lax.rem(s + N_SEQ - 1, N_SEQ))

    def chain_copy(d, c):
        return rcopy(cs.at[d, c], cr.at[d, c], c_ss.at[d, c], c_rs.at[d, c], seq=nexts[d])

    def chain(p):
        for d in range(SIDES):
            c = p - LAG * places[d]

            @pl.when((c >= 0) & (c < CHUNKS) & (places[d] < N_SEQ - 1))
            def _():
                @pl.when(places[d] > 0)
                def _():
                    chain_copy(d, c).wait_recv()
                    cs[d, c] = (
                        cs[d, c].astype(f32) + keeps[d] * cr[d, c].astype(f32)).astype(bf16)

                chain_copy(d, c).start()

    chain(0)
    ring_step(1, 1)

    def part_tile(i, _):
        m = lax.div(i, 4)
        side = lax.rem(lax.div(i, 2), 2)
        group = lax.rem(i, 2)

        @pl.when((lax.rem(i, 2) == 0) & (i > 0))
        def _():
            chain(lax.div(i, 2))

        for n, (j, mm) in ((2, (2, 0)), (4, (2, 1)), (7, (3, 0))):
            @pl.when(i == n)
            def _():
                ring_step(j, mm)

        low_m = low_t[rank_rows(m), :]
        left = jnp.concatenate([low_m * mask_of(side, group * 4 + k) for k in range(4)], axis=0)
        p = jnp.dot(left, xg[m, :, half_rows(side)], preferred_element_type=f32)
        parts[m, half_rows(group), half_rows(side)] = p.astype(bf16)
        return 0

    lax.fori_loop(0, 8, part_tile, 0)
    chain(4)
    ring_step(3, 1)

    def fix(i, _):
        rows = pl.ds(pl.multiple_of(i * TILE, TILE), TILE)
        h = lax.div(i, 2)
        sub = pl.ds(pl.multiple_of(lax.rem(i, 2) * TILE, TILE), TILE)
        corr = lax.dot_general(low[h, 0, sub, :], ab[1], NT, preferred_element_type=f32)
        out_ref[rows, :] = (acc[rows, :] + SCALE * corr).astype(bf16)
        return 0

    lax.fori_loop(0, BLK // TILE, fix, 0)
    chain(5)

    ring_wait(3, 0)
    ring_wait(3, 1)
    ld_q.wait()
    ld_r.wait()
    r = rv[...]
    r_hi = r.astype(bf16)
    r_lo = (r - r_hi.astype(f32)).astype(bf16)
    r2 = jnp.concatenate([r_hi, r_lo], axis=0)

    go = []
    for k in range(TOUCH):
        e = jnp.minimum(first_id + k, EX - 1)
        done = (k <= n_slots) & (bounds[1, e] <= low_pos + BLK)
        left_go = jnp.where(done, owner[0, e], -1)
        e = jnp.maximum(last_id - k, 0)
        done = (k <= n_slots) & (bounds[0, e] >= low_pos)
        go.append((left_go, jnp.where(done, owner[0, e], -1)))

    def widths(side, lo, n):
        u = uv[side, lo * 64:(lo + n) * 64, :]
        return jnp.dot(u, qv[side * WIDE:(side + 1) * WIDE, :], preferred_element_type=f32)

    def feature_rows(f):
        return jnp.concatenate([f[:KR] + f[KR:2 * KR], f[2 * KR:3 * KR] + f[3 * KR:]], axis=0)

    def normalized(i, _):
        k = lax.rem(lax.div(i, 2) + 1, TOUCH)
        m = lax.rem(i, 2)
        for n, p in ((4, 6), (8, 7)):
            @pl.when(i == n)
            def _():
                chain(p)

        @pl.when(i == 14)
        def _():
            for d in range(SIDES):
                @pl.when(places[d] == N_SEQ - 1)
                def _():
                    for c in range(CHUNKS):
                        chain_copy(d, c).wait_recv()

            for d in range(SIDES):
                cc = slice(d * WIDE, (d + 1) * WIDE)
                for c in range(CHUNKS):
                    rr = slice((c % 2) * 64, (c % 2) * 64 + 64)
                    parts[c // 2, rr, cc] = (
                        parts[c // 2, rr, cc].astype(f32)
                        + begins[d] * cr[d, c].astype(f32)).astype(bf16)

        for c in range(COLS // TILE):
            cc = slice(c * TILE, (c + 1) * TILE)
            rows = []
            for z in range(N_Z):
                a = mom[m, z, 0, :, cc].astype(f32)
                b = mom[m, z, 1, :, cc].astype(f32)
                m1 = jnp.concatenate([a[:8], b[:8]], axis=0)
                m2 = jnp.concatenate([a[8:], b[8:]], axis=0)
                g = parts[m, pl.ds(pl.multiple_of(k * RANK + z * 16, 16), 16), cc].astype(f32)
                first = BETA_ONE * m1 + (1.0 - BETA_ONE) * g
                second = BETA_TWO * m2 + (1.0 - BETA_TWO) * (g * g)
                root = second * lax.rsqrt(second) + EPSILON
                rows.append((first * lax.rsqrt(root * root)).astype(bf16))
            u = jnp.dot(r2, jnp.concatenate(rows, axis=0), preferred_element_type=f32)
            u = u[:KR] + u[KR:]
            hi = u.astype(bf16)
            side = c // 2
            uc = slice((c % 2) * TILE, (c % 2) * TILE + TILE)
            uv[side, pl.ds(pl.multiple_of(i * 32, 32), 16), uc] = hi
            uv[side, pl.ds(pl.multiple_of(i * 32 + 16, 16), 16), uc] = (
                u - hi.astype(f32)).astype(bf16)
        return 0

    lax.fori_loop(0, 2 * TOUCH, normalized, 0)

    fs = [[None] * TOUCH, [None] * TOUCH]
    for d in range(SIDES):
        f = widths(d, 0, TOUCH)
        for kk in range(TOUCH):
            facc[d, kk] = feature_rows(f[kk * 64:(kk + 1) * 64])

    def place(o, _):
        total = jnp.zeros((2 * KR, KD), f32)
        for k in range(TOUCH):
            for d in range(SIDES):
                total = total + jnp.where(go[k][d] == o, 1.0, 0.0) * facc[d, (k + TOUCH - 1) % TOUCH]
        fsend[o] = total.astype(bf16)
        return 0

    lax.fori_loop(0, GROUP, place, 0)

    def feature_copy(o, j):
        return rcopy(
            fsend.at[o], frecv.at[me], f_ss.at[j], f_rs.at[me],
            seq=lax.div(o, N_TP), tensor=lax.rem(o, N_TP))

    def send_out(j, _):
        feature_copy(lax.rem(me + j, GROUP), j).start()
        return 0

    lax.fori_loop(1, GROUP, send_out, 0)
    frecv[me] = fsend[me]

    def arrive(j, _):
        o = lax.rem(me + j, GROUP)
        rcopy(fsend.at[o], frecv.at[o], f_ss.at[j], f_rs.at[o],
              seq=lax.div(o, N_TP), tensor=lax.rem(o, N_TP)).wait_recv()
        return 0

    lax.fori_loop(1, GROUP, arrive, 0)

    def add(o, total):
        return total + frecv[o].astype(f32)

    feat = lax.fori_loop(0, GROUP, add, jnp.zeros((2 * KR, KD), f32))
    feat_ref[pl.ds(0, 2 * KR, stride=2), :] = feat[:, :128]
    feat_ref[pl.ds(1, 2 * KR, stride=2), :] = feat[:, 128:]

    ex1.wait_send()
    ex2.wait_send()
    ex3.wait_send()
    for m in range(2):
        mx(m, xh).wait_send()
        for j in range(4):
            for c in ring(j, m, 0):
                c.wait_send()

    for d in range(SIDES):
        @pl.when(places[d] < N_SEQ - 1)
        def _():
            for c in range(CHUNKS):
                chain_copy(d, c).wait_send()

    def left(j, _):
        feature_copy(lax.rem(me + j, GROUP), j).wait_send()
        return 0

    lax.fori_loop(1, GROUP, left, 0)


def per_device(x, g, a, b, w, m1, m2, r, q, bounds, owner):
    hbm = pl.BlockSpec(memory_space=pltpu.HBM)
    vmem = pl.BlockSpec(memory_space=pltpu.VMEM)
    dma = pltpu.SemaphoreType.DMA
    V = pltpu.VMEM
    att, feat = pl.pallas_call(
        kernel,
        out_shape=(
            jax.ShapeDtypeStruct((BLK, COLS), bf16),
            jax.ShapeDtypeStruct((4 * KR, KD // 2), f32),
        ),
        in_specs=[hbm] * 11,
        out_specs=(vmem, vmem),
        scratch_shapes=[
            V((2, BLK, COLS), bf16), V((BLK, WIDTH), bf16), V((COLS, WIDTH), bf16),
            V((2, COLS, RANK), bf16), V((RANK, COLS), bf16), V((COLS, KD), bf16),
            V((2, 8, COLS), f32), V((2, 8, COLS), f32), V((KR, RANK), f32),
            pltpu.SMEM((2, EX), jnp.int32), pltpu.SMEM((1, EX), jnp.int32),
            V((BLK, COLS), f32),
            V((2, HALF, RANK), bf16), V((2, HALF, RANK), bf16), V((2, HALF, RANK), f32),
            V((2, HALF, RANK), bf16), V((2, HALF, RANK), bf16),
            V((2, 2, HALF, RANK), bf16), V((2 * RANK, BLK), bf16),
            V((2, TOUCH * RANK, COLS), bf16),
            V((SIDES, CHUNKS, 64, WIDE), bf16), V((SIDES, CHUNKS, 64, WIDE), bf16),
            V((2, N_Z, 2, 16, COLS), bf16),
            V((SIDES, TOUCH * 64, WIDE), bf16), V((SIDES, TOUCH, 2 * KR, KD), f32),
            V((GROUP, 2 * KR, KD), bf16), V((GROUP, 2 * KR, KD), bf16),
            dma((18,)), dma((3,)), dma((3,)), dma((2,)), dma((2,)),
            dma((4, 2, 2)), dma((4, 2, 2)), dma((SIDES, CHUNKS)), dma((SIDES, CHUNKS)),
            dma((GROUP,)), dma((GROUP,)),
        ],
        compiler_params=pltpu.CompilerParams(
            collective_id=0, has_side_effects=True, vmem_limit_bytes=VLIMIT * 2**20),
        name="step",
    )(
        x.reshape(BLK, COLS), g.reshape(BLK, WIDTH), a, b, w, m1, m2, r, q,
        bounds.reshape(2, EX), owner.reshape(1, EX),
    )
    return att.reshape(1, BLK, COLS), feat.reshape(1, 1, 2 * KR * KD)


def solution(mesh):
    return jax.shard_map(
        per_device,
        mesh=mesh,
        in_specs=(
            P("dp", "seq", "tensor"),
            P("dp", "seq", None),
            P("tensor", None),
            P(None, "tensor"),
            P("tensor", None),
            P(None, "dp", "tensor"),
            P(None, "dp", "tensor"),
            P(),
            P(),
            P("dp", None, None),
            P("dp", None),
        ),
        out_specs=(P("dp", "seq", "tensor"), P("dp", ("seq", "tensor"), None)),
        check_vma=False,
    )
```

```python
import jax
import jax.numpy as jnp
from jax import lax
from jax.experimental import pallas as pl
from jax.experimental.pallas import tpu as pltpu
from jax.sharding import PartitionSpec as P

TOUCH = 8
SCALE = 4.0
BETA_ONE = 0.9
BETA_TWO = 0.999
EPSILON = 1e-08

N_DP, N_SEQ, N_TP = 16, 4, 4
GROUP = N_SEQ * N_TP
BLK = 1024
WIDTH = 4096
COLS = WIDTH // N_TP
RANK = 128
KR, KD = 16, 256
EX = 16
HALF = BLK // 2
TILE = 256
WIDE = 512
CHUNKS = 4
SIDES = 2
N_Z = 8
VLIMIT = 60

bf16 = jnp.bfloat16
f32 = jnp.float32
NT = (((1,), (1,)), ((), ()))
MESH_ID = pl.DeviceIdType.MESH


def kernel(
    x_hbm, g_hbm, a_hbm, b_hbm, w_hbm, m1_hbm, m2_hbm, r_hbm, q_hbm, bounds_hbm, owner_hbm,
    out_hbm, feat_ref,
    xg, gv, wv, ab, bv, qv, m1v, m2v, rv, bounds, owner, acc, outv,
    ex1s, ex1r, lowh, ex2s, ex2r, low, low_t, parts, cs, cr, mom, uv, fv, facc, fsend, frecv,
    ld_sem, out_sem, ex_ss, ex_rs, mx_ss, mx_rs, mz_ss, mz_rs, c_ss, c_rs, f_ss, f_rs,
):
    dp = lax.axis_index("dp")
    s = lax.axis_index("seq")
    t = lax.axis_index("tensor")
    core = lax.rem(t, 2)
    chip = lax.div(t, 2)
    partner = chip * 2 + (1 - core)
    across = (1 - chip) * 2 + core
    zi = lax.div(dp, 2)
    xh = lax.rem(dp, 2)
    xpeer = zi * 2 + (1 - xh)
    zright = lax.rem(zi + 1, N_Z)
    zleft = lax.rem(zi + N_Z - 1, N_Z)
    me = s * N_TP + t

    def col(i):
        return pl.ds(pl.multiple_of(lax.rem(t + i, N_TP) * COLS, COLS), COLS)

    def half_rows(h):
        return pl.ds(pl.multiple_of(h * HALF, HALF), HALF)

    def load(i, src, dst):
        return pltpu.make_async_copy(src, dst, ld_sem.at[i])

    ld_m1 = load(0, m1_hbm, m1v)
    ld_m2 = load(1, m2_hbm, m2v)
    ld_a = load(2, a_hbm, ab.at[1])
    ld_b = load(3, b_hbm, bv)
    ld_low = [
        load(4 + i, x_hbm.at[half_rows(h), :], xg.at[0, half_rows(h), :])
        for i, h in enumerate((1 - core, core))
    ] + [
        load(6 + i, g_hbm.at[half_rows(h), col(0)], xg.at[1, half_rows(h), :])
        for i, h in enumerate((1 - core, core))
    ]
    ld_g = [
        [load(8 + 4 * h + i, g_hbm.at[half_rows(h), col(i)], gv.at[half_rows(h), col(i)])
         for i in range(1, N_TP)] for h in range(2)
    ]
    own_g = [load(8 + 4 * h, xg.at[1, half_rows(h), :], gv.at[half_rows(h), col(0)])
             for h in range(2)]
    ld_w = [
        load(16 + i, w_hbm.at[pl.ds(i * WIDE, WIDE), :], wv.at[pl.ds(i * WIDE, WIDE), :])
        for i in range(2)
    ]
    ld_q = load(18, q_hbm.at[col(0), :], qv)
    ld_r = load(19, r_hbm, rv)
    ld_bounds = load(20, bounds_hbm, bounds)
    ld_owner = load(21, owner_hbm, owner)
    for c in (ld_m1, ld_m2, ld_a, ld_low[0], ld_low[1], ld_b, ld_low[2], ld_low[3], *ld_g[0],
              ld_w[0], *ld_g[1], ld_w[1], ld_q, ld_r, ld_bounds, ld_owner):
        c.start()

    barrier = pltpu.get_barrier_semaphore()

    def greet(j, _):
        o = lax.rem(me + j, GROUP)
        pl.semaphore_signal(
            barrier, inc=1, device_id={"seq": lax.div(o, N_TP), "tensor": lax.rem(o, N_TP)},
            device_id_type=MESH_ID)
        return 0

    lax.fori_loop(1, GROUP, greet, 0)
    for peer in (xpeer, zright * 2 + xh, zleft * 2 + xh):
        pl.semaphore_signal(barrier, inc=1, device_id={"dp": peer}, device_id_type=MESH_ID)

    def rcopy(src, dst, ss, rs, **where):
        return pltpu.make_async_remote_copy(
            src_ref=src, dst_ref=dst, send_sem=ss, recv_sem=rs, device_id=where,
            device_id_type=MESH_ID)

    def ex1(m):
        return rcopy(ex1s.at[m], ex1r.at[m], ex_ss.at[0, m], ex_rs.at[0, m], tensor=partner)

    def ex2(m):
        return rcopy(ex2s.at[m], ex2r.at[m], ex_ss.at[1, m], ex_rs.at[1, m], tensor=across)

    def ex3(m, half):
        return rcopy(low.at[half, m], low.at[half, m], ex_ss.at[2, m], ex_rs.at[2, m],
                     tensor=partner)

    def second(m):
        ex1(m).wait_recv()
        total = lowh[m] + ex1r[m].astype(f32)
        lowh[m] = total
        ex2s[m] = total.astype(bf16)
        ex2(m).start()

    def third(m):
        ex2(m).wait_recv()
        low[core, m] = (lowh[m] + ex2r[m].astype(f32)).astype(bf16)
        ex3(m, core).start()

    def mx(m, block):
        return rcopy(mom.at[m, zi, xh], mom.at[m, zi, block], mx_ss.at[m], mx_rs.at[m], dp=xpeer)

    right_dp = zright * 2 + xh
    left_dp = zleft * 2 + xh

    def ring(j, m, ahead):
        zr = lax.rem(zi + N_Z - j - ahead, N_Z)
        zl = lax.rem(zi + j + ahead, N_Z)
        if j < 3:
            a = mom.at[m, zr]
            b = mom.at[m, zl]
        else:
            a = mom.at[m, zr, 0]
            b = mom.at[m, zl, 1]
        return (
            rcopy(a, a, mz_ss.at[j, m, 0], mz_rs.at[j, m, 0], dp=right_dp),
            rcopy(b, b, mz_ss.at[j, m, 1], mz_rs.at[j, m, 1], dp=left_dp),
        )

    def ring_wait(j, m):
        for c in ring(j, m, 1):
            c.wait_recv()

    def ring_step(j, m):
        if j == 0:
            mx(m, 1 - xh).wait_recv()
        else:
            ring_wait(j - 1, m)
        for c in ring(j, m, 0):
            c.start()

    ld_a.wait()

    def partial(i, _):
        m = 1 - lax.div(i, 2)
        late = lax.rem(i, 2)
        rows = half_rows(jnp.where(late == 1, core, 1 - core))

        @pl.when(i == 2)
        def _():
            ld_b.wait()
            ab[0] = bv[...].T

        for n in range(4):
            @pl.when(i == n)
            def _():
                ld_low[n].wait()

        p = jnp.dot(xg[1 - m, rows, :], ab[m], preferred_element_type=f32)

        @pl.when(late == 0)
        def _():
            ex1s[m] = p.astype(bf16)

        @pl.when(late == 1)
        def _():
            lowh[m] = p

        @pl.when(i == 0)
        def _():
            pl.semaphore_wait(barrier, GROUP - 1 + 3)
            ex1(1).start()
            ld_m1.wait()
            ld_m2.wait()
            for mm in range(2):
                mom[mm, zi, xh] = jnp.concatenate([m1v[mm], m2v[mm]], axis=0).astype(bf16)
                mx(mm, xh).start()

        @pl.when(i == 2)
        def _():
            ex1(0).start()

        return 0

    lax.fori_loop(0, 4, partial, 0)
    for c in own_g:
        c.start()
    second(1)

    for c in ld_g[0]:
        c.wait()
    own_g[0].wait()
    ld_w[0].wait()
    second(0)

    def main_tile(i, _):
        @pl.when(i == 1)
        def _():
            for c in ld_g[1]:
                c.wait()
            own_g[1].wait()
            ring_step(0, 0)
            ring_step(0, 1)

        @pl.when(i == 2)
        def _():
            ld_w[1].wait()
            third(1)

        rows = half_rows(lax.rem(i, 2))
        cc = pl.ds(pl.multiple_of(lax.div(i, 2) * WIDE, WIDE), WIDE)
        acc[rows, cc] = lax.dot_general(
            gv[rows, :], wv[cc, :], NT, preferred_element_type=f32)
        return 0

    lax.fori_loop(0, 3, main_tile, 0)

    third(0)
    ring_step(1, 0)

    ld_bounds.wait()
    ld_owner.wait()
    low_pos = s * BLK
    n_le = jnp.int32(0)
    n_lt = jnp.int32(0)
    n_last = jnp.int32(0)
    n_next = jnp.int32(0)
    pos = low_pos + lax.broadcasted_iota(jnp.int32, (1, BLK), 1)
    ids = jnp.full((1, BLK), -1, jnp.int32)
    for e in range(EX):
        st = bounds[0, e]
        n_le = n_le + (st <= low_pos).astype(jnp.int32)
        n_lt = n_lt + (st < low_pos).astype(jnp.int32)
        n_last = n_last + (st <= low_pos + BLK - 1).astype(jnp.int32)
        n_next = n_next + (st <= low_pos + BLK).astype(jnp.int32)
        ids = ids + (st <= pos).astype(jnp.int32)
    first_id = n_le - 1
    last_id = n_last - 1
    n_slots = last_id - first_id
    single = (first_id == last_id).astype(f32)
    inside = (s < N_SEQ - 1).astype(jnp.int32)
    from_left = (n_le == n_lt).astype(f32)
    from_right = ((n_next == n_last).astype(jnp.int32) * inside).astype(f32)
    begins = (from_left, from_right)
    keeps = (from_left * single, from_right * single)

    def mask_of(side, k):
        slot = jnp.where(side == 0, ids - first_id, last_id - ids)
        return (slot == k).astype(f32).astype(bf16)

    def rank_rows(m):
        return pl.ds(pl.multiple_of(m * RANK, RANK), RANK)

    places = (s, N_SEQ - 1 - s)
    nexts = (lax.rem(s + 1, N_SEQ), lax.rem(s + N_SEQ - 1, N_SEQ))

    def chain_copy(d, c):
        return rcopy(cs.at[d, c], cr.at[d, c], c_ss.at[d, c], c_rs.at[d, c], seq=nexts[d])

    def chain(place, c):
        for d in range(SIDES):
            @pl.when(places[d] == place)
            def _():
                if place > 0:
                    chain_copy(d, c).wait_recv()
                    cs[d, c] = (
                        cs[d, c].astype(f32) + keeps[d] * cr[d, c].astype(f32)).astype(bf16)
                chain_copy(d, c).start()

    def far(i, _):
        m = 1 - lax.div(i, 2)
        side = lax.rem(i, 2)

        for mm in (1, 0):
            @pl.when(i == 2 * (1 - mm))
            def _():
                if mm == 0:
                    chain(0, 0)
                    chain(0, 1)
                    ring_step(1, 1)
                ex3(mm, 1 - core).wait_recv()

        @pl.when(side == 0)
        def _():
            for h in range(2):
                low_t[rank_rows(m), h * HALF:(h + 1) * HALF] = (
                    low[h, m].astype(f32) * SCALE).T.astype(bf16)

        left = low_t[rank_rows(m), :] * mask_of(side, n_slots)
        p = jnp.dot(left, xg[m, :, half_rows(side)], preferred_element_type=f32).astype(bf16)
        cs[side, 2 - 2 * m] = p[:64]
        cs[side, 3 - 2 * m] = p[64:]
        return 0

    lax.fori_loop(0, 4, far, 0)
    chain(0, 2)
    chain(0, 3)

    @pl.when(s == 0)
    def _():
        cr[0] = jnp.zeros((CHUNKS, 64, WIDE), bf16)

    @pl.when(s == N_SEQ - 1)
    def _():
        cr[1] = jnp.zeros((CHUNKS, 64, WIDE), bf16)

    def part_tile(i, _):
        m = lax.div(i, 4)
        side = lax.rem(lax.div(i, 2), 2)
        group = lax.rem(i, 2)

        for n, steps in (
            (1, ((2, 0),)), (4, ((2, 1),)), (6, ((3, 0),)),
        ):
            @pl.when(i == n)
            def _():
                for j, mm in steps:
                    ring_step(j, mm)

        for n, steps in (
            (3, ((1, 0),)), (5, ((1, 1),)), (7, ((1, 2), (2, 0))),
        ):
            @pl.when(i == n)
            def _():
                for place, c in steps:
                    chain(place, c)

        low_m = low_t[rank_rows(m), :]
        left = jnp.concatenate([low_m * mask_of(side, group * 4 + k) for k in range(4)], axis=0)
        p = jnp.dot(left, xg[m, :, half_rows(side)], preferred_element_type=f32)
        parts[m, half_rows(group), half_rows(side)] = p.astype(bf16)
        return 0

    lax.fori_loop(0, 8, part_tile, 0)
    ring_step(3, 1)

    ld_q.wait()
    ld_r.wait()
    ring_wait(3, 0)
    r = rv[...]
    r_hi = r.astype(bf16)
    r_lo = (r - r_hi.astype(f32)).astype(bf16)
    r2 = jnp.concatenate([r_hi, r_lo], axis=0)

    go = []
    for k in range(TOUCH):
        e = jnp.minimum(first_id + k, EX - 1)
        done = (k <= n_slots) & (bounds[1, e] <= low_pos + BLK)
        left_go = jnp.where(done, owner[0, e], -1)
        e = jnp.maximum(last_id - k, 0)
        done = (k <= n_slots) & (bounds[0, e] >= low_pos)
        go.append((left_go, jnp.where(done, owner[0, e], -1)))

    def widths(side, lo, n):
        u = uv[side, lo * 64:(lo + n) * 64, :]
        f = jnp.dot(u, qv[side * WIDE:(side + 1) * WIDE, :], preferred_element_type=f32)
        for i in range(n):
            v = f[i * 64:(i + 1) * 64]
            fv[side, lo + i] = jnp.concatenate(
                [v[:KR] + v[KR:2 * KR], v[2 * KR:3 * KR] + v[3 * KR:]], axis=0)

    def placed(o, total, slots):
        for k in slots:
            for d in range(SIDES):
                total = total + jnp.where(go[k][d] == o, 1.0, 0.0) * fv[d, (k + TOUCH - 1) % TOUCH]
        return total

    def normalized(i, _):
        early = i < 2 * (TOUCH - 1)
        m = jnp.where(early, lax.div(i, TOUCH - 1), i - 2 * (TOUCH - 1))
        k = jnp.where(early, lax.rem(i, TOUCH - 1) + 1, 0)
        row = jnp.where(early, k - 1, TOUCH - 1) * 64 + m * 32
        for n, steps in (
            (0, ((1, 3), (2, 1))), (3, ((2, 2),)), (6, ((2, 3),)),
        ):
            @pl.when(i == n)
            def _():
                for place, c in steps:
                    chain(place, c)

        @pl.when(i == TOUCH - 1)
        def _():
            ring_wait(3, 1)

        @pl.when(i == 2 * (TOUCH - 1))
        def _():
            for d in range(SIDES):
                widths(d, 0, TOUCH - 1)

            def place_most(o, _):
                facc[o] = placed(o, jnp.zeros((2 * KR, KD), f32), range(1, TOUCH))
                return 0

            lax.fori_loop(0, GROUP, place_most, 0)
            for d in range(SIDES):
                @pl.when(places[d] == N_SEQ - 1)
                def _():
                    for c in range(CHUNKS):
                        chain_copy(d, c).wait_recv()

            for d in range(SIDES):
                cc = slice(d * WIDE, (d + 1) * WIDE)
                for c in range(CHUNKS):
                    rr = slice((c % 2) * 64, (c % 2) * 64 + 64)
                    parts[1 - c // 2, rr, cc] = (
                        parts[1 - c // 2, rr, cc].astype(f32)
                        + begins[d] * cr[d, c].astype(f32)).astype(bf16)

        for c in range(COLS // TILE):
            cc = slice(c * TILE, (c + 1) * TILE)
            rows = []
            for z in range(N_Z):
                a = mom[m, z, 0, :, cc].astype(f32)
                b = mom[m, z, 1, :, cc].astype(f32)
                m1 = jnp.concatenate([a[:8], b[:8]], axis=0)
                m2 = jnp.concatenate([a[8:], b[8:]], axis=0)
                g = parts[m, pl.ds(pl.multiple_of(k * RANK + z * 16, 16), 16), cc].astype(f32)
                first = BETA_ONE * m1 + (1.0 - BETA_ONE) * g
                second = BETA_TWO * m2 + (1.0 - BETA_TWO) * (g * g)
                root = second * lax.rsqrt(second) + EPSILON
                rows.append((first * lax.rsqrt(root * root)).astype(bf16))
            u = jnp.dot(r2, jnp.concatenate(rows, axis=0), preferred_element_type=f32)
            u = u[:KR] + u[KR:]
            hi = u.astype(bf16)
            side = c // 2
            uc = slice((c % 2) * TILE, (c % 2) * TILE + TILE)
            uv[side, pl.ds(pl.multiple_of(row, 32), 16), uc] = hi
            uv[side, pl.ds(pl.multiple_of(row + 16, 16), 16), uc] = (
                u - hi.astype(f32)).astype(bf16)
        return 0

    lax.fori_loop(0, 2 * TOUCH, normalized, 0)

    for d in range(SIDES):
        widths(d, TOUCH - 1, 1)

    def feature_copy(o):
        return rcopy(
            fsend.at[o], frecv.at[me], f_ss.at[o], f_rs.at[me],
            seq=lax.div(o, N_TP), tensor=lax.rem(o, N_TP))

    def place(j, _):
        o = lax.rem(me + 1 + j, GROUP)
        fsend[o] = placed(o, facc[o], (0,)).astype(bf16)

        @pl.when(j < GROUP - 1)
        def _():
            feature_copy(o).start()

        return 0

    lax.fori_loop(0, GROUP, place, 0)
    frecv[me] = fsend[me]

    lax.fori_loop(3, 4, main_tile, 0)

    def out_copy(i):
        rows = pl.ds(pl.multiple_of(i * TILE, TILE), TILE)
        return pltpu.make_async_copy(outv.at[rows, :], out_hbm.at[rows, :], out_sem.at[i])

    def fix(i, _):
        rows = pl.ds(pl.multiple_of(i * TILE, TILE), TILE)
        h = lax.div(i, 2)
        sub = pl.ds(pl.multiple_of(lax.rem(i, 2) * TILE, TILE), TILE)
        corr = lax.dot_general(low[h, 0, sub, :], ab[1], NT, preferred_element_type=f32)
        outv[rows, :] = (acc[rows, :] + SCALE * corr).astype(bf16)
        out_copy(i).start()
        return 0

    lax.fori_loop(0, BLK // TILE, fix, 0)

    def arrive(j, _):
        o = lax.rem(me + j, GROUP)
        rcopy(fsend.at[o], frecv.at[o], f_ss.at[o], f_rs.at[o],
              seq=lax.div(o, N_TP), tensor=lax.rem(o, N_TP)).wait_recv()
        return 0

    lax.fori_loop(1, GROUP, arrive, 0)

    def add(o, total):
        return total + frecv[o].astype(f32)

    feat = lax.fori_loop(0, GROUP, add, jnp.zeros((2 * KR, KD), f32))
    feat_ref[pl.ds(0, 2 * KR, stride=2), :] = feat[:, :128]
    feat_ref[pl.ds(1, 2 * KR, stride=2), :] = feat[:, 128:]

    for m in range(2):
        ex1(m).wait_send()
        ex2(m).wait_send()
        ex3(m, core).wait_send()
        mx(m, xh).wait_send()
        for j in range(4):
            for c in ring(j, m, 0):
                c.wait_send()

    for d in range(SIDES):
        @pl.when(places[d] < N_SEQ - 1)
        def _():
            for c in range(CHUNKS):
                chain_copy(d, c).wait_send()

    def left(j, _):
        feature_copy(lax.rem(me + j, GROUP)).wait_send()
        return 0

    lax.fori_loop(1, GROUP, left, 0)
    for i in range(BLK // TILE):
        out_copy(i).wait()


def per_device(x, g, a, b, w, m1, m2, r, q, bounds, owner):
    any_ = pl.BlockSpec(memory_space=pl.ANY)
    vmem = pl.BlockSpec(memory_space=pltpu.VMEM)
    dma = pltpu.SemaphoreType.DMA
    V = pltpu.VMEM
    att, feat = pl.pallas_call(
        kernel,
        out_shape=(
            jax.ShapeDtypeStruct((BLK, COLS), bf16),
            jax.ShapeDtypeStruct((4 * KR, KD // 2), f32),
        ),
        in_specs=[any_] * 11,
        out_specs=(any_, vmem),
        scratch_shapes=[
            V((2, BLK, COLS), bf16), V((BLK, WIDTH), bf16), V((COLS, WIDTH), bf16),
            V((2, COLS, RANK), bf16), V((RANK, COLS), bf16), V((COLS, KD), bf16),
            V((2, 8, COLS), f32), V((2, 8, COLS), f32), V((KR, RANK), f32),
            pltpu.SMEM((2, EX), jnp.int32), pltpu.SMEM((1, EX), jnp.int32),
            V((BLK, COLS), f32), V((BLK, COLS), bf16),
            V((2, HALF, RANK), bf16), V((2, HALF, RANK), bf16), V((2, HALF, RANK), f32),
            V((2, HALF, RANK), bf16), V((2, HALF, RANK), bf16),
            V((2, 2, HALF, RANK), bf16), V((2 * RANK, BLK), bf16),
            V((2, TOUCH * RANK, COLS), bf16),
            V((SIDES, CHUNKS, 64, WIDE), bf16), V((SIDES, CHUNKS, 64, WIDE), bf16),
            V((2, N_Z, 2, 16, COLS), bf16),
            V((SIDES, TOUCH * 64, WIDE), bf16), V((SIDES, TOUCH, 2 * KR, KD), f32),
            V((GROUP, 2 * KR, KD), f32),
            V((GROUP, 2 * KR, KD), bf16), V((GROUP, 2 * KR, KD), bf16),
            dma((22,)), dma((4,)), dma((3, 2)), dma((3, 2)), dma((2,)), dma((2,)),
            dma((4, 2, 2)), dma((4, 2, 2)), dma((SIDES, CHUNKS)), dma((SIDES, CHUNKS)),
            dma((GROUP,)), dma((GROUP,)),
        ],
        compiler_params=pltpu.CompilerParams(
            collective_id=0, has_side_effects=True, vmem_limit_bytes=VLIMIT * 2**20),
        name="step",
    )(
        x.reshape(BLK, COLS), g.reshape(BLK, WIDTH), a, b, w, m1, m2, r, q,
        bounds.reshape(2, EX), owner.reshape(1, EX),
    )
    return att.reshape(1, BLK, COLS), feat.reshape(1, 1, 2 * KR * KD)


def solution(mesh):
    return jax.shard_map(
        per_device,
        mesh=mesh,
        in_specs=(
            P("dp", "seq", "tensor"),
            P("dp", "seq", None),
            P("tensor", None),
            P(None, "tensor"),
            P("tensor", None),
            P(None, "dp", "tensor"),
            P(None, "dp", "tensor"),
            P(),
            P(),
            P("dp", None, None),
            P("dp", None),
        ),
        out_specs=(P("dp", "seq", "tensor"), P("dp", ("seq", "tensor"), None)),
        check_vma=False,
    )
```

```python
import jax
import jax.numpy as jnp
from jax import lax
from jax.experimental import pallas as pl
from jax.experimental.pallas import tpu as pltpu
from jax.sharding import PartitionSpec as P

TOUCH = 8
SCALE = 4.0
BETA_ONE = 0.9
BETA_TWO = 0.999
EPSILON = 1e-08

N_DP, N_SEQ, N_TP = 16, 4, 4
GROUP = N_SEQ * N_TP
BLK = 1024
WIDTH = 4096
COLS = WIDTH // N_TP
RANK = 128
KR, KD = 16, 256
EX = 16
HALF = BLK // 2
TILE = 256
WIDE = 512
CHUNKS = 8
SLICE = 32
SIDES = 2
N_Z = 8
VLIMIT = 60
PIECES = 8

bf16 = jnp.bfloat16
f32 = jnp.float32
NT = (((1,), (1,)), ((), ()))
MESH_ID = pl.DeviceIdType.MESH


def kernel(
    x_hbm, g_hbm, a_hbm, b_hbm, w_hbm, m1_hbm, m2_hbm, r_hbm, q_hbm, bounds_hbm, owner_hbm,
    out_hbm, frecv,
    xg, gv, wv, ab, bv, qv, m1v, m2v, rv, bounds, owner, acc, outv,
    ex1s, ex1r, lowh, ex2s, ex2r, low, low_t, parts, cs, cr, mom, scaled, uv, fv, facc, fsend,
    ld_sem, out_sem, ex_ss, ex_rs, mx_ss, mx_rs, za_ss, za_rs, zb_ss, zb_rs, c_ss, c_rs, f_ss, f_rs,
):
    dp = lax.axis_index("dp")
    s = lax.axis_index("seq")
    t = lax.axis_index("tensor")
    core = lax.rem(t, 2)
    chip = lax.div(t, 2)
    partner = chip * 2 + (1 - core)
    across = (1 - chip) * 2 + core
    zi = lax.div(dp, 2)
    xh = lax.rem(dp, 2)
    xpeer = zi * 2 + (1 - xh)
    z_steps = (1, 2, N_Z - 1, N_Z - 2)
    z_peers = [lax.rem(zi + d, N_Z) * 2 + xh for d in z_steps]
    me = s * N_TP + t

    def col(i):
        return pl.ds(pl.multiple_of(lax.rem(t + i, N_TP) * COLS, COLS), COLS)

    def half_rows(h):
        return pl.ds(pl.multiple_of(h * HALF, HALF), HALF)

    def load(i, src, dst):
        return pltpu.make_async_copy(src, dst, ld_sem.at[i])

    ld_m1 = load(0, m1_hbm, m1v)
    ld_m2 = load(1, m2_hbm, m2v)
    ld_a = load(2, a_hbm, ab.at[1])
    ld_b = load(3, b_hbm, bv)
    ld_low = [
        load(4 + i, x_hbm.at[half_rows(h), :], xg.at[0, half_rows(h), :])
        for i, h in enumerate((1 - core, core))
    ] + [
        load(6 + i, g_hbm.at[half_rows(h), col(0)], xg.at[1, half_rows(h), :])
        for i, h in enumerate((1 - core, core))
    ]
    ld_g = [
        [load(8 + 4 * h + i, g_hbm.at[half_rows(h), col(i)], gv.at[half_rows(h), col(i)])
         for i in range(1, N_TP)] for h in range(2)
    ]
    own_g = [load(8 + 4 * h, xg.at[1, half_rows(h), :], gv.at[half_rows(h), col(0)])
             for h in range(2)]
    ld_w = [
        load(16 + i, w_hbm.at[pl.ds(i * WIDE, WIDE), :], wv.at[pl.ds(i * WIDE, WIDE), :])
        for i in range(2)
    ]
    ld_q = load(20, q_hbm.at[col(0), :], qv)
    ld_r = load(21, r_hbm, rv)
    ld_bounds = load(22, bounds_hbm, bounds)
    ld_owner = load(23, owner_hbm, owner)
    for c in (ld_m1, ld_m2, ld_a, ld_low[0], ld_low[1], ld_b, ld_low[2], ld_low[3], *ld_g[0],
              ld_w[0], *ld_g[1], *ld_w[1:], ld_q, ld_r, ld_bounds, ld_owner):
        c.start()

    barrier = pltpu.get_barrier_semaphore()

    def greet(j, _):
        o = lax.rem(me + j, GROUP)
        pl.semaphore_signal(
            barrier, inc=1, device_id={"seq": lax.div(o, N_TP), "tensor": lax.rem(o, N_TP)},
            device_id_type=MESH_ID)
        return 0

    lax.fori_loop(1, GROUP, greet, 0)
    for peer in (xpeer, *z_peers):
        pl.semaphore_signal(barrier, inc=1, device_id={"dp": peer}, device_id_type=MESH_ID)

    def rcopy(src, dst, ss, rs, **where):
        return pltpu.make_async_remote_copy(
            src_ref=src, dst_ref=dst, send_sem=ss, recv_sem=rs, device_id=where,
            device_id_type=MESH_ID)

    def ex1(m):
        return rcopy(ex1s.at[m], ex1r.at[m], ex_ss.at[0, m], ex_rs.at[0, m], tensor=partner)

    def ex2(m):
        return rcopy(ex2s.at[m], ex2r.at[m], ex_ss.at[1, m], ex_rs.at[1, m], tensor=across)

    def ex3(m, half):
        return rcopy(low.at[half, m], low.at[half, m], ex_ss.at[2, m], ex_rs.at[2, m],
                     tensor=partner)

    def second(m):
        ex1(m).wait_recv()
        total = lowh[m] + ex1r[m].astype(f32)
        lowh[m] = total
        ex2s[m] = total.astype(bf16)
        ex2(m).start()

    def third(m):
        ex2(m).wait_recv()
        low[core, m] = (lowh[m] + ex2r[m].astype(f32)).astype(bf16)
        ex3(m, core).start()

    sides_x = (xh, 1 - xh)

    def mx(x):
        return rcopy(mom.at[zi, xh], mom.at[zi, x], mx_ss, mx_rs, dp=xpeer)

    def near_copy(a, i):
        block = mom.at[zi, sides_x[a]]
        return rcopy(block, block, za_ss.at[a, i], za_rs.at[a, i], dp=z_peers[i])

    def near_wait(a, i):
        block = mom.at[lax.rem(zi + N_Z - z_steps[i], N_Z), sides_x[a]]
        rcopy(block, block, za_ss.at[a, i], za_rs.at[a, i], dp=z_peers[i]).wait_recv()

    def far_block(a, i, hops):
        d = z_steps[i] if i < 2 else z_steps[i] - N_Z
        side = 1 if d > 0 else -1
        z = lax.rem(zi + 2 * N_Z - side * hops, N_Z)
        x = sides_x[a]
        if d in (1, -1):
            return mom.at[z, x]
        return mom.at[z, x, 0 if d > 0 else 1]

    def far_copy(a, i):
        block = far_block(a, i, 2)
        return rcopy(block, block, zb_ss.at[a, i], zb_rs.at[a, i], dp=z_peers[i])

    def far_wait(a, i):
        block = far_block(a, i, 3 + i % 2)
        rcopy(block, block, zb_ss.at[a, i], zb_rs.at[a, i], dp=z_peers[i]).wait_recv()

    def round_one(a):
        if a == 1:
            mx(1 - xh).wait_recv()
        for i in range(4):
            near_copy(a, i).start()

    def round_two(a):
        for i in (1, 3):
            near_wait(a, i)
        for i in range(4):
            far_copy(a, i).start()

    ld_a.wait()

    def partial(i, _):
        m = 1 - lax.div(i, 2)
        late = lax.rem(i, 2)
        rows = half_rows(jnp.where(late == 1, core, 1 - core))

        @pl.when(i == 2)
        def _():
            ld_b.wait()
            ab[0] = bv[...].T

        for n in range(4):
            @pl.when(i == n)
            def _():
                ld_low[n].wait()

        p = jnp.dot(xg[1 - m, rows, :], ab[m], preferred_element_type=f32)

        @pl.when(late == 0)
        def _():
            ex1s[m] = p.astype(bf16)

        @pl.when(late == 1)
        def _():
            lowh[m] = p

        @pl.when(i == 0)
        def _():
            pl.semaphore_wait(barrier, GROUP - 1 + 5)
            ex1(1).start()
            ld_m1.wait()
            ld_m2.wait()
            for mm in range(2):
                mom[zi, xh, mm] = jnp.concatenate([m1v[mm], m2v[mm]], axis=0).astype(bf16)
            mx(xh).start()
            round_one(0)

        @pl.when(i == 2)
        def _():
            ex1(0).start()

        return 0

    lax.fori_loop(0, 4, partial, 0)
    for c in own_g:
        c.start()
    second(1)

    for c in ld_g[0]:
        c.wait()
    own_g[0].wait()
    ld_w[0].wait()
    second(0)

    def main_tile(i, _):
        @pl.when(i == 1)
        def _():
            for c in ld_g[1]:
                c.wait()
            own_g[1].wait()

        @pl.when(i == 1)
        def _():
            round_one(1)

        @pl.when(i == 2)
        def _():
            ld_w[1].wait()
            third(1)
            round_two(0)

        rows = half_rows(lax.rem(i, 2))
        cc = pl.ds(pl.multiple_of(lax.div(i, 2) * WIDE, WIDE), WIDE)
        acc[rows, cc] = lax.dot_general(
            gv[rows, :], wv[cc, :], NT, preferred_element_type=f32)
        return 0

    lax.fori_loop(0, 3, main_tile, 0)

    third(0)

    ld_bounds.wait()
    ld_owner.wait()
    low_pos = s * BLK
    n_le = jnp.int32(0)
    n_lt = jnp.int32(0)
    n_last = jnp.int32(0)
    n_next = jnp.int32(0)
    pos = low_pos + lax.broadcasted_iota(jnp.int32, (1, BLK), 1)
    ids = jnp.full((1, BLK), -1, jnp.int32)
    for e in range(EX):
        st = bounds[0, e]
        n_le = n_le + (st <= low_pos).astype(jnp.int32)
        n_lt = n_lt + (st < low_pos).astype(jnp.int32)
        n_last = n_last + (st <= low_pos + BLK - 1).astype(jnp.int32)
        n_next = n_next + (st <= low_pos + BLK).astype(jnp.int32)
        ids = ids + (st <= pos).astype(jnp.int32)
    first_id = n_le - 1
    last_id = n_last - 1
    n_slots = last_id - first_id
    single = (first_id == last_id).astype(f32)
    inside = (s < N_SEQ - 1).astype(jnp.int32)
    from_left = (n_le == n_lt).astype(f32)
    from_right = ((n_next == n_last).astype(jnp.int32) * inside).astype(f32)
    begins = (from_left, from_right)
    keeps = (from_left * single, from_right * single)

    def mask_of(side, k):
        slot = jnp.where(side == 0, ids - first_id, last_id - ids)
        return (slot == k).astype(f32).astype(bf16)

    def rank_rows(m):
        return pl.ds(pl.multiple_of(m * RANK, RANK), RANK)

    places = (s, N_SEQ - 1 - s)
    nexts = (lax.rem(s + 1, N_SEQ), lax.rem(s + N_SEQ - 1, N_SEQ))

    def chain_copy(d, c):
        return rcopy(cs.at[d, c], cr.at[d, c], c_ss.at[d, c], c_rs.at[d, c], seq=nexts[d])

    def chain(place, c):
        for d in range(SIDES):
            @pl.when(places[d] == place)
            def _():
                if place > 0:
                    chain_copy(d, c).wait_recv()
                    cs[d, c] = (
                        cs[d, c].astype(f32) + keeps[d] * cr[d, c].astype(f32)).astype(bf16)
                chain_copy(d, c).start()

    def far(i, _):
        m = 1 - lax.div(i, 2)
        side = lax.rem(i, 2)

        for mm in (1, 0):
            @pl.when(i == 2 * (1 - mm))
            def _():
                if mm == 0:
                    for c in range(CHUNKS // 2):
                        chain(0, c)
                ex3(mm, 1 - core).wait_recv()

        @pl.when(side == 0)
        def _():
            for h in range(2):
                low_t[rank_rows(m), h * HALF:(h + 1) * HALF] = (
                    low[h, m].astype(f32) * SCALE).T.astype(bf16)

        left = low_t[rank_rows(m), :] * mask_of(side, n_slots)
        p = jnp.dot(left, xg[m, :, half_rows(side)], preferred_element_type=f32).astype(bf16)
        for c in range(CHUNKS // 2):
            cs[side, (1 - m) * (CHUNKS // 2) + c] = p[c * SLICE:(c + 1) * SLICE]
        return 0

    lax.fori_loop(0, 4, far, 0)
    for c in range(CHUNKS // 2, CHUNKS):
        chain(0, c)
    round_two(1)

    @pl.when(s == 0)
    def _():
        cr[0] = jnp.zeros((CHUNKS, SLICE, WIDE), bf16)

    @pl.when(s == N_SEQ - 1)
    def _():
        cr[1] = jnp.zeros((CHUNKS, SLICE, WIDE), bf16)

    def part_tile(i, _):
        m = lax.div(i, 4)
        side = lax.rem(lax.div(i, 2), 2)
        group = lax.rem(i, 2)

        for n, steps in (
            (3, ((1, 0),)), (4, ((1, 1),)), (5, ((1, 2),)), (6, ((1, 3),)),
            (7, ((1, 4), (2, 0))),
        ):
            @pl.when(i == n)
            def _():
                for place, c in steps:
                    chain(place, c)

        low_m = low_t[rank_rows(m), :]
        left = jnp.concatenate([low_m * mask_of(side, group * 4 + k) for k in range(4)], axis=0)
        p = jnp.dot(left, xg[m, :, half_rows(side)], preferred_element_type=f32)
        parts[m, half_rows(group), half_rows(side)] = p.astype(bf16)
        return 0

    lax.fori_loop(0, 8, part_tile, 0)
    chain(1, 5)
    chain(2, 1)

    for a in range(2):
        for i in (0, 2):
            near_wait(a, i)
        for i in range(4):
            far_wait(a, i)
    ld_q.wait()
    ld_r.wait()
    r = rv[...]
    r_hi = r.astype(bf16)
    r_lo = (r - r_hi.astype(f32)).astype(bf16)
    r2 = jnp.concatenate([r_hi, r_lo], axis=0)

    go = []
    for k in range(TOUCH):
        e = jnp.minimum(first_id + k, EX - 1)
        done = (k <= n_slots) & (bounds[1, e] <= low_pos + BLK)
        left_go = jnp.where(done, owner[0, e], -1)
        e = jnp.maximum(last_id - k, 0)
        done = (k <= n_slots) & (bounds[0, e] >= low_pos)
        go.append((left_go, jnp.where(done, owner[0, e], -1)))

    def widths(side, lo, n):
        u = uv[side, lo * 64:(lo + n) * 64, :]
        f = jnp.dot(u, qv[side * WIDE:(side + 1) * WIDE, :], preferred_element_type=f32)
        for i in range(n):
            v = f[i * 64:(i + 1) * 64]
            fv[side, lo + i] = jnp.concatenate(
                [v[:KR] + v[KR:2 * KR], v[2 * KR:3 * KR] + v[3 * KR:]], axis=0)

    def placed(o, total, slots):
        for k in slots:
            for d in range(SIDES):
                total = total + jnp.where(go[k][d] == o, 1.0, 0.0) * fv[d, (k + TOUCH - 1) % TOUCH]
        return total

    def moments_of(m, z, cc):
        a = mom[z, 0, m, :, cc].astype(f32)
        b = mom[z, 1, m, :, cc].astype(f32)
        return (
            BETA_ONE * jnp.concatenate([a[:8], b[:8]], axis=0),
            BETA_TWO * jnp.concatenate([a[8:], b[8:]], axis=0),
        )

    def normalize(scaled, g):
        first = scaled[0] + (1.0 - BETA_ONE) * g
        second = scaled[1] + (1.0 - BETA_TWO) * (g * g)
        root = second * lax.rsqrt(second) + EPSILON
        return (first * lax.rsqrt(root * root)).astype(bf16)

    def rank_side(k, m, side, n):
        row = (k + TOUCH - 1) % TOUCH * 64 + m * 32
        u = jnp.dot(r2, n, preferred_element_type=f32)
        u = u[:KR] + u[KR:]
        hi = u.astype(bf16)
        uv[side, pl.ds(pl.multiple_of(row, 32), 16), :] = hi
        uv[side, pl.ds(pl.multiple_of(row + 16, 16), 16), :] = (u - hi.astype(f32)).astype(bf16)

    def scale_moments(m, side):
        cc = half_rows(side)
        for z in range(N_Z):
            for i, v in enumerate(moments_of(m, z, cc)):
                scaled[i, z * 16:z * 16 + 16, :] = v

    def seven(i, _):
        m = lax.rem(i, 2)
        side = lax.div(i, 2)
        for n, steps in (
            (0, ((1, 6), (2, 2))), (1, ((1, 7), (2, 3))), (2, ((2, 4),)), (3, ((2, 5),)),
        ):
            @pl.when(i == n)
            def _():
                for place, c in steps:
                    chain(place, c)

        scale_moments(m, side)
        for k in range(1, TOUCH):
            g = parts[m, k * RANK:(k + 1) * RANK, half_rows(side)].astype(f32)
            rank_side(k, m, side, normalize((scaled[0], scaled[1]), g))
        return 0

    lax.fori_loop(0, 4, seven, 0)
    chain(2, 6)
    chain(2, 7)

    for d in range(SIDES):
        widths(d, 0, TOUCH - 1)

    def place_most(o, _):
        facc[o] = placed(o, jnp.zeros((2 * KR, KD), f32), range(1, TOUCH))
        return 0

    lax.fori_loop(0, GROUP, place_most, 0)

    for d in range(SIDES):
        @pl.when(places[d] == N_SEQ - 1)
        def _():
            for c in range(CHUNKS):
                chain_copy(d, c).wait_recv()

    def slot_zero(i, _):
        m = lax.rem(i, 2)
        side = lax.div(i, 2)
        scale_moments(m, side)
        begin = jnp.where(side == 0, begins[0], begins[1])
        came = jnp.concatenate(
            [cr[side, (1 - m) * (CHUNKS // 2) + c].astype(f32) for c in range(CHUNKS // 2)], axis=0)
        g = parts[m, :RANK, half_rows(side)].astype(f32) + begin * came
        rank_side(0, m, side, normalize((scaled[0], scaled[1]), g))
        return 0

    lax.fori_loop(0, 4, slot_zero, 0)

    for d in range(SIDES):
        widths(d, TOUCH - 1, 1)

    def feature_copy(o):
        return rcopy(
            fsend.at[o], frecv.at[me], f_ss.at[o], f_rs.at[me],
            seq=lax.div(o, N_TP), tensor=lax.rem(o, N_TP))

    def place(j, _):
        o = lax.rem(me + 1 + j, GROUP)
        fsend[o] = placed(o, facc[o], (0,)).astype(bf16)

        @pl.when(j < GROUP - 1)
        def _():
            feature_copy(o).start()

        return 0

    lax.fori_loop(0, GROUP, place, 0)
    own_feature = pltpu.make_async_copy(fsend.at[me], frecv.at[me], f_ss.at[me])
    own_feature.start()

    lax.fori_loop(3, 4, main_tile, 0)

    def out_copy(i):
        rows = pl.ds(pl.multiple_of(i * TILE, TILE), TILE)
        return pltpu.make_async_copy(outv.at[rows, :], out_hbm.at[rows, :], out_sem.at[i])

    def fix(i, _):
        rows = pl.ds(pl.multiple_of(i * TILE, TILE), TILE)
        h = lax.div(i, 2)
        sub = pl.ds(pl.multiple_of(lax.rem(i, 2) * TILE, TILE), TILE)
        corr = lax.dot_general(low[h, 0, sub, :], ab[1], NT, preferred_element_type=f32)
        outv[rows, :] = (acc[rows, :] + SCALE * corr).astype(bf16)
        out_copy(i).start()
        return 0

    lax.fori_loop(0, BLK // TILE, fix, 0)

    def arrive(j, _):
        o = lax.rem(me + j, GROUP)
        rcopy(fsend.at[o], frecv.at[o], f_ss.at[o], f_rs.at[o],
              seq=lax.div(o, N_TP), tensor=lax.rem(o, N_TP)).wait_recv()
        return 0

    lax.fori_loop(1, GROUP, arrive, 0)

    for m in range(2):
        ex1(m).wait_send()
        ex2(m).wait_send()
        ex3(m, core).wait_send()
    mx(xh).wait_send()
    for a in range(2):
        for i in range(4):
            near_copy(a, i).wait_send()
            far_copy(a, i).wait_send()

    for d in range(SIDES):
        @pl.when(places[d] < N_SEQ - 1)
        def _():
            for c in range(CHUNKS):
                chain_copy(d, c).wait_send()

    def left(j, _):
        feature_copy(lax.rem(me + j, GROUP)).wait_send()
        return 0

    lax.fori_loop(1, GROUP, left, 0)
    own_feature.wait()
    for i in range(BLK // TILE):
        out_copy(i).wait()


def finish(att_in, feat_in, att_out, feat_out, buf, fbuf, fsum, in_sem, out_sem, f_in, f_out):
    def piece(i):
        return pl.ds(i * (BLK // PIECES), BLK // PIECES)

    def load(i):
        return pltpu.make_async_copy(att_in.at[piece(i), :], buf.at[piece(i), :], in_sem.at[i])

    def store(i):
        return pltpu.make_async_copy(buf.at[piece(i), :], att_out.at[piece(i), :], out_sem.at[i])

    features = pltpu.make_async_copy(feat_in, fbuf, f_in)
    features.start()
    for i in range(PIECES):
        load(i).start()
    for i in range(PIECES):
        load(i).wait()
        store(i).start()
    features.wait()

    def add(o, total):
        return total + fbuf[o].astype(f32)

    feat = lax.fori_loop(0, GROUP, add, jnp.zeros((2 * KR, KD), f32))
    fsum[pl.ds(0, 2 * KR, stride=2), :] = feat[:, :128]
    fsum[pl.ds(1, 2 * KR, stride=2), :] = feat[:, 128:]
    result = pltpu.make_async_copy(fsum, feat_out, f_out)
    result.start()
    result.wait()
    for i in range(PIECES):
        store(i).wait()


def per_device(x, g, a, b, w, m1, m2, r, q, bounds, owner):
    any_ = pl.BlockSpec(memory_space=pl.ANY)
    dma = pltpu.SemaphoreType.DMA
    V = pltpu.VMEM
    att, arrived = pl.pallas_call(
        kernel,
        out_shape=(
            jax.ShapeDtypeStruct((BLK, COLS), bf16),
            jax.ShapeDtypeStruct((GROUP, 2 * KR, KD), bf16),
        ),
        in_specs=[any_] * 11,
        out_specs=(any_, any_),
        scratch_shapes=[
            V((2, BLK, COLS), bf16), V((BLK, WIDTH), bf16), V((COLS, WIDTH), bf16),
            V((2, COLS, RANK), bf16), V((RANK, COLS), bf16), V((COLS, KD), bf16),
            V((2, 8, COLS), f32), V((2, 8, COLS), f32), V((KR, RANK), f32),
            pltpu.SMEM((2, EX), jnp.int32), pltpu.SMEM((1, EX), jnp.int32),
            V((BLK, COLS), f32), V((BLK, COLS), bf16),
            V((2, HALF, RANK), bf16), V((2, HALF, RANK), bf16), V((2, HALF, RANK), f32),
            V((2, HALF, RANK), bf16), V((2, HALF, RANK), bf16),
            V((2, 2, HALF, RANK), bf16), V((2 * RANK, BLK), bf16),
            V((2, TOUCH * RANK, COLS), bf16),
            V((SIDES, CHUNKS, SLICE, WIDE), bf16), V((SIDES, CHUNKS, SLICE, WIDE), bf16),
            V((N_Z, 2, 2, 16, COLS), bf16), V((2, RANK, WIDE), f32),
            V((SIDES, TOUCH * 64, WIDE), bf16), V((SIDES, TOUCH, 2 * KR, KD), f32),
            V((GROUP, 2 * KR, KD), f32),
            V((GROUP, 2 * KR, KD), bf16),
            dma((24,)), dma((4,)), dma((3, 2)), dma((3, 2)), dma(()), dma(()),
            dma((2, 4)), dma((2, 4)), dma((2, 4)), dma((2, 4)), dma((SIDES, CHUNKS)), dma((SIDES, CHUNKS)),
            dma((GROUP,)), dma((GROUP,)),
        ],
        compiler_params=pltpu.CompilerParams(
            collective_id=0, has_side_effects=True, vmem_limit_bytes=VLIMIT * 2**20),
        name="step",
    )(
        x.reshape(BLK, COLS), g.reshape(BLK, WIDTH), a, b, w, m1, m2, r, q,
        bounds.reshape(2, EX), owner.reshape(1, EX),
    )
    att, feat = pl.pallas_call(
        finish,
        out_shape=(
            jax.ShapeDtypeStruct((BLK, COLS), bf16),
            jax.ShapeDtypeStruct((4 * KR, KD // 2), f32),
        ),
        in_specs=[any_, any_],
        out_specs=(any_, any_),
        scratch_shapes=[
            V((BLK, COLS), bf16), V((GROUP, 2 * KR, KD), bf16), V((4 * KR, KD // 2), f32),
            dma((PIECES,)), dma((PIECES,)), dma(()), dma(()),
        ],
        compiler_params=pltpu.CompilerParams(vmem_limit_bytes=VLIMIT * 2**20),
        name="finish",
    )(att, arrived)
    return att.reshape(1, BLK, COLS), feat.reshape(1, 1, 2 * KR * KD)


def solution(mesh):
    return jax.shard_map(
        per_device,
        mesh=mesh,
        in_specs=(
            P("dp", "seq", "tensor"),
            P("dp", "seq", None),
            P("tensor", None),
            P(None, "tensor"),
            P("tensor", None),
            P(None, "dp", "tensor"),
            P(None, "dp", "tensor"),
            P(),
            P(),
            P("dp", None, None),
            P("dp", None),
        ),
        out_specs=(P("dp", "seq", "tensor"), P("dp", ("seq", "tensor"), None)),
        check_vma=False,
    )
```

```python
import jax
import jax.numpy as jnp
from jax import lax
from jax.experimental import pallas as pl
from jax.experimental.pallas import tpu as pltpu
from jax.sharding import PartitionSpec as P

TOUCH = 8
SCALE = 4.0
BETA_ONE = 0.9
BETA_TWO = 0.999
EPSILON = 1e-08

N_DP, N_SEQ, N_TP = 16, 4, 4
GROUP = N_SEQ * N_TP
BLK = 1024
WIDTH = 4096
COLS = WIDTH // N_TP
RANK = 128
KR, KD = 16, 256
EX = 16
HALF = BLK // 2
TILE = 256
WIDE = 512
CHUNKS = 8
SLICE = 32
SIDES = 2
N_Z = 8
VLIMIT = 60
PIECES = 8

bf16 = jnp.bfloat16
f32 = jnp.float32
NT = (((1,), (1,)), ((), ()))
MESH_ID = pl.DeviceIdType.MESH


def kernel(
    x_hbm, g_hbm, a_hbm, b_hbm, w_hbm, m1_hbm, m2_hbm, r_hbm, q_hbm, bounds_hbm, owner_hbm,
    out_hbm, frecv,
    xg, gv, wv, ab, bv, qv, m1v, m2v, rv, bounds, owner, acc, outv,
    ex1s, ex1r, lowh, ex2s, ex2r, low, low_t, parts, cs, cr, mom, scaled, uv, fv, facc, fsend,
    ld_sem, out_sem, ex_ss, ex_rs, mx_ss, mx_rs, za_ss, za_rs, zb_ss, zb_rs, c_ss, c_rs, f_ss, f_rs,
):
    dp = lax.axis_index("dp")
    s = lax.axis_index("seq")
    t = lax.axis_index("tensor")
    core = lax.rem(t, 2)
    chip = lax.div(t, 2)
    partner = chip * 2 + (1 - core)
    across = (1 - chip) * 2 + core
    zi = lax.div(dp, 2)
    xh = lax.rem(dp, 2)
    xpeer = zi * 2 + (1 - xh)
    z_steps = (1, 2, N_Z - 1, N_Z - 2)
    z_peers = [lax.rem(zi + d, N_Z) * 2 + xh for d in z_steps]
    me = s * N_TP + t

    def col(i):
        return pl.ds(pl.multiple_of(lax.rem(t + i, N_TP) * COLS, COLS), COLS)

    def half_rows(h):
        return pl.ds(pl.multiple_of(h * HALF, HALF), HALF)

    def load(i, src, dst):
        return pltpu.make_async_copy(src, dst, ld_sem.at[i])

    ld_m1 = load(0, m1_hbm, m1v)
    ld_m2 = load(1, m2_hbm, m2v)
    ld_a = load(2, a_hbm, ab.at[1])
    ld_b = load(3, b_hbm, bv)
    ld_low = [
        load(4 + i, x_hbm.at[half_rows(h), :], xg.at[0, half_rows(h), :])
        for i, h in enumerate((1 - core, core))
    ] + [
        load(6 + i, g_hbm.at[half_rows(h), col(0)], xg.at[1, half_rows(h), :])
        for i, h in enumerate((1 - core, core))
    ]
    ld_g = [
        [load(8 + 4 * h + i, g_hbm.at[half_rows(h), col(i)], gv.at[half_rows(h), col(i)])
         for i in range(1, N_TP)] for h in range(2)
    ]
    own_g = [load(8 + 4 * h, xg.at[1, half_rows(h), :], gv.at[half_rows(h), col(0)])
             for h in range(2)]
    ld_w = [
        load(16 + i, w_hbm.at[pl.ds(i * TILE, TILE), :], wv.at[pl.ds(i * TILE, TILE), :])
        for i in range(4)
    ]
    ld_q = load(20, q_hbm.at[col(0), :], qv)
    ld_r = load(21, r_hbm, rv)
    ld_bounds = load(22, bounds_hbm, bounds)
    ld_owner = load(23, owner_hbm, owner)
    for c in (ld_m1, ld_m2, ld_a, ld_low[0], ld_low[1], ld_b, ld_low[2], ld_low[3], *ld_g[0],
              ld_w[0], *ld_g[1], *ld_w[1:], ld_q, ld_r, ld_bounds, ld_owner):
        c.start()

    barrier = pltpu.get_barrier_semaphore()

    def greet(j, _):
        o = lax.rem(me + j, GROUP)
        pl.semaphore_signal(
            barrier, inc=1, device_id={"seq": lax.div(o, N_TP), "tensor": lax.rem(o, N_TP)},
            device_id_type=MESH_ID)
        return 0

    lax.fori_loop(1, GROUP, greet, 0)
    for peer in (xpeer, *z_peers):
        pl.semaphore_signal(barrier, inc=1, device_id={"dp": peer}, device_id_type=MESH_ID)

    def rcopy(src, dst, ss, rs, **where):
        return pltpu.make_async_remote_copy(
            src_ref=src, dst_ref=dst, send_sem=ss, recv_sem=rs, device_id=where,
            device_id_type=MESH_ID)

    def ex1(m):
        return rcopy(ex1s.at[m], ex1r.at[m], ex_ss.at[0, m], ex_rs.at[0, m], tensor=partner)

    def ex2(m):
        return rcopy(ex2s.at[m], ex2r.at[m], ex_ss.at[1, m], ex_rs.at[1, m], tensor=across)

    def ex3(m, half):
        return rcopy(low.at[half, m], low.at[half, m], ex_ss.at[2, m], ex_rs.at[2, m],
                     tensor=partner)

    def second(m):
        ex1(m).wait_recv()
        total = lowh[m] + ex1r[m].astype(f32)
        lowh[m] = total
        ex2s[m] = total.astype(bf16)
        ex2(m).start()

    def third(m):
        ex2(m).wait_recv()
        low[core, m] = (lowh[m] + ex2r[m].astype(f32)).astype(bf16)
        ex3(m, core).start()

    sides_x = (xh, 1 - xh)

    def mx(x):
        return rcopy(mom.at[zi, xh], mom.at[zi, x], mx_ss, mx_rs, dp=xpeer)

    def near_copy(a, i):
        block = mom.at[zi, sides_x[a]]
        return rcopy(block, block, za_ss.at[a, i], za_rs.at[a, i], dp=z_peers[i])

    def near_wait(a, i):
        block = mom.at[lax.rem(zi + N_Z - z_steps[i], N_Z), sides_x[a]]
        rcopy(block, block, za_ss.at[a, i], za_rs.at[a, i], dp=z_peers[i]).wait_recv()

    def far_block(a, i, hops):
        d = z_steps[i] if i < 2 else z_steps[i] - N_Z
        side = 1 if d > 0 else -1
        z = lax.rem(zi + 2 * N_Z - side * hops, N_Z)
        x = sides_x[a]
        if d in (1, -1):
            return mom.at[z, x]
        return mom.at[z, x, 0 if d > 0 else 1]

    def far_copy(a, i):
        block = far_block(a, i, 2)
        return rcopy(block, block, zb_ss.at[a, i], zb_rs.at[a, i], dp=z_peers[i])

    def far_wait(a, i):
        block = far_block(a, i, 3 + i % 2)
        rcopy(block, block, zb_ss.at[a, i], zb_rs.at[a, i], dp=z_peers[i]).wait_recv()

    def round_one(a):
        if a == 1:
            mx(1 - xh).wait_recv()
        for i in range(4):
            near_copy(a, i).start()

    def round_two(a):
        for i in (1, 3):
            near_wait(a, i)
        for i in range(4):
            far_copy(a, i).start()

    ld_b.wait()
    ab[0] = bv[...].T
    ld_m1.wait()
    ld_m2.wait()
    for mm in range(2):
        mom[zi, xh, mm] = jnp.concatenate([m1v[mm], m2v[mm]], axis=0).astype(bf16)
    ld_a.wait()

    def partial(i, _):
        m = 1 - lax.div(i, 2)
        late = lax.rem(i, 2)
        rows = half_rows(jnp.where(late == 1, core, 1 - core))

        for n in range(4):
            @pl.when(i == n)
            def _():
                ld_low[n].wait()

        p = jnp.dot(xg[1 - m, rows, :], ab[m], preferred_element_type=f32)

        @pl.when(late == 0)
        def _():
            ex1s[m] = p.astype(bf16)

        @pl.when(late == 1)
        def _():
            lowh[m] = p

        @pl.when(i == 1)
        def _():
            pl.semaphore_wait(barrier, GROUP - 1 + 5)
            ex1(1).start()
            mx(xh).start()
            round_one(0)

        @pl.when(i == 2)
        def _():
            ex1(0).start()

        return 0

    lax.fori_loop(0, 4, partial, 0)
    for c in own_g:
        c.start()
    second(1)

    for c in ld_g[0]:
        c.wait()
    own_g[0].wait()
    ld_w[0].wait()
    second(0)

    ld_bounds.wait()
    ld_owner.wait()
    low_pos = s * BLK
    n_le = jnp.int32(0)
    n_lt = jnp.int32(0)
    n_last = jnp.int32(0)
    n_next = jnp.int32(0)
    pos = low_pos + lax.broadcasted_iota(jnp.int32, (1, BLK), 1)
    ids = jnp.full((1, BLK), -1, jnp.int32)
    for e in range(EX):
        st = bounds[0, e]
        n_le = n_le + (st <= low_pos).astype(jnp.int32)
        n_lt = n_lt + (st < low_pos).astype(jnp.int32)
        n_last = n_last + (st <= low_pos + BLK - 1).astype(jnp.int32)
        n_next = n_next + (st <= low_pos + BLK).astype(jnp.int32)
        ids = ids + (st <= pos).astype(jnp.int32)
    first_id = n_le - 1
    last_id = n_last - 1
    n_slots = last_id - first_id
    single = (first_id == last_id).astype(f32)
    inside = (s < N_SEQ - 1).astype(jnp.int32)
    from_left = (n_le == n_lt).astype(f32)
    from_right = ((n_next == n_last).astype(jnp.int32) * inside).astype(f32)
    begins = (from_left, from_right)
    keeps = (from_left * single, from_right * single)

    def mask_of(side, k):
        slot = jnp.where(side == 0, ids - first_id, last_id - ids)
        return (slot == k).astype(f32).astype(bf16)

    def rank_rows(m):
        return pl.ds(pl.multiple_of(m * RANK, RANK), RANK)

    places = (s, N_SEQ - 1 - s)
    nexts = (lax.rem(s + 1, N_SEQ), lax.rem(s + N_SEQ - 1, N_SEQ))

    def chain_copy(d, c):
        return rcopy(cs.at[d, c], cr.at[d, c], c_ss.at[d, c], c_rs.at[d, c], seq=nexts[d])

    def chain(place, c):
        for d in range(SIDES):
            @pl.when(places[d] == place)
            def _():
                if place > 0:
                    chain_copy(d, c).wait_recv()
                    cs[d, c] = (
                        cs[d, c].astype(f32) + keeps[d] * cr[d, c].astype(f32)).astype(bf16)
                chain_copy(d, c).start()

    def far(m):
        ex3(m, 1 - core).wait_recv()
        for h in range(2):
            low_t[m * RANK:(m + 1) * RANK, h * HALF:(h + 1) * HALF] = (
                low[h, m].astype(f32) * SCALE).T.astype(bf16)

        def one(side, _):
            left = low_t[m * RANK:(m + 1) * RANK, :] * mask_of(side, n_slots)
            p = jnp.dot(left, xg[m, :, half_rows(side)], preferred_element_type=f32).astype(bf16)
            for c in range(CHUNKS // 2):
                cs[side, (1 - m) * (CHUNKS // 2) + c] = p[c * SLICE:(c + 1) * SLICE]
            return 0

        lax.fori_loop(0, SIDES, one, 0)
        for c in range(CHUNKS // 2):
            chain(0, (1 - m) * (CHUNKS // 2) + c)

    def main_tile(i, _):
        @pl.when(i == 1)
        def _():
            for c in ld_g[1]:
                c.wait()
            own_g[1].wait()

        for n in (1, 2, 3):
            @pl.when(i == 2 * n)
            def _():
                ld_w[n].wait()

        @pl.when(i == 3)
        def _():
            round_one(1)

        @pl.when(i == 4)
        def _():
            third(1)

        @pl.when(i == 5)
        def _():
            far(1)
            third(0)
            round_two(0)

        rows = half_rows(lax.rem(i, 2))
        cc = pl.ds(pl.multiple_of(lax.div(i, 2) * TILE, TILE), TILE)
        acc[rows, cc] = lax.dot_general(
            gv[rows, :], wv[cc, :], NT, preferred_element_type=f32)
        return 0

    lax.fori_loop(0, 6, main_tile, 0)

    far(0)

    @pl.when(s == 0)
    def _():
        cr[0] = jnp.zeros((CHUNKS, SLICE, WIDE), bf16)

    @pl.when(s == N_SEQ - 1)
    def _():
        cr[1] = jnp.zeros((CHUNKS, SLICE, WIDE), bf16)

    def part_tile(i, _):
        m = lax.div(i, 4)
        side = lax.rem(lax.div(i, 2), 2)
        group = lax.rem(i, 2)

        for n, steps in (
            (1, ((1, 0),)), (2, ((1, 1),)), (3, ((1, 2),)), (4, ((1, 3),)),
            (5, ((1, 4), (2, 0))), (6, ((1, 5), (2, 1))), (7, ((1, 6), (2, 2))),
        ):
            @pl.when(i == n)
            def _():
                for place, c in steps:
                    chain(place, c)

        @pl.when(i == 2)
        def _():
            round_two(1)

        low_m = low_t[rank_rows(m), :]
        left = jnp.concatenate([low_m * mask_of(side, group * 4 + k) for k in range(4)], axis=0)
        p = jnp.dot(left, xg[m, :, half_rows(side)], preferred_element_type=f32)
        parts[m, half_rows(group), half_rows(side)] = p.astype(bf16)
        return 0

    lax.fori_loop(0, 8, part_tile, 0)
    chain(1, 7)
    chain(2, 3)

    for a in range(2):
        for i in (0, 2):
            near_wait(a, i)
        for i in range(4):
            far_wait(a, i)
    ld_q.wait()
    ld_r.wait()
    r = rv[...]
    r_hi = r.astype(bf16)
    r_lo = (r - r_hi.astype(f32)).astype(bf16)
    r2 = jnp.concatenate([r_hi, r_lo], axis=0)

    go = []
    for k in range(TOUCH):
        e = jnp.minimum(first_id + k, EX - 1)
        done = (k <= n_slots) & (bounds[1, e] <= low_pos + BLK)
        left_go = jnp.where(done, owner[0, e], -1)
        e = jnp.maximum(last_id - k, 0)
        done = (k <= n_slots) & (bounds[0, e] >= low_pos)
        go.append((left_go, jnp.where(done, owner[0, e], -1)))

    def widths(side, lo, n):
        u = uv[side, lo * 64:(lo + n) * 64, :]
        f = jnp.dot(u, qv[side * WIDE:(side + 1) * WIDE, :], preferred_element_type=f32)
        for i in range(n):
            v = f[i * 64:(i + 1) * 64]
            fv[side, lo + i] = jnp.concatenate(
                [v[:KR] + v[KR:2 * KR], v[2 * KR:3 * KR] + v[3 * KR:]], axis=0)

    def placed(o, total, slots):
        for k in slots:
            for d in range(SIDES):
                total = total + jnp.where(go[k][d] == o, 1.0, 0.0) * fv[d, (k + TOUCH - 1) % TOUCH]
        return total

    def moments_of(m, z, cc):
        a = mom[z, 0, m, :, cc].astype(f32)
        b = mom[z, 1, m, :, cc].astype(f32)
        return (
            BETA_ONE * jnp.concatenate([a[:8], b[:8]], axis=0),
            BETA_TWO * jnp.concatenate([a[8:], b[8:]], axis=0),
        )

    def normalize(scaled, g):
        first = scaled[0] + (1.0 - BETA_ONE) * g
        second = scaled[1] + (1.0 - BETA_TWO) * (g * g)
        root = second * lax.rsqrt(second) + EPSILON
        return (first * lax.rsqrt(root * root)).astype(bf16)

    def rank_side(k, m, side, n):
        row = (k + TOUCH - 1) % TOUCH * 64 + m * 32
        u = jnp.dot(r2, n, preferred_element_type=f32)
        u = u[:KR] + u[KR:]
        hi = u.astype(bf16)
        if not isinstance(row, int):
            row = pl.multiple_of(row, 32)
        uv[side, pl.ds(row, 16), :] = hi
        uv[side, pl.ds(row + 16, 16), :] = (u - hi.astype(f32)).astype(bf16)

    def scale_moments(m, side):
        cc = half_rows(side)
        for z in range(N_Z):
            for i, v in enumerate(moments_of(m, z, cc)):
                scaled[2 * side + m, i, z * 16:z * 16 + 16, :] = v

    def seven(i, _):
        m = lax.rem(i, 2)
        side = lax.div(i, 2)
        for n, steps in (
            (0, ((2, 4),)), (1, ((2, 5),)), (2, ((2, 6), (2, 7))),
        ):
            @pl.when(i == n)
            def _():
                for place, c in steps:
                    chain(place, c)

        scale_moments(m, side)
        for k in range(1, TOUCH):
            g = parts[m, k * RANK:(k + 1) * RANK, half_rows(side)].astype(f32)
            rank_side(k, m, side, normalize((scaled[i, 0], scaled[i, 1]), g))
        return 0

    lax.fori_loop(0, 4, seven, 0)

    for d in range(SIDES):
        widths(d, 0, TOUCH - 1)

    def place_most(o, _):
        facc[o] = placed(o, jnp.zeros((2 * KR, KD), f32), range(1, TOUCH))
        return 0

    lax.fori_loop(0, GROUP, place_most, 0)

    for d in range(SIDES):
        @pl.when(places[d] == N_SEQ - 1)
        def _():
            for c in range(CHUNKS):
                chain_copy(d, c).wait_recv()

    for i in range(4):
        m = i % 2
        side = i // 2
        came = jnp.concatenate(
            [cr[side, (1 - m) * (CHUNKS // 2) + c].astype(f32) for c in range(CHUNKS // 2)], axis=0)
        g = parts[m, :RANK, side * WIDE:(side + 1) * WIDE].astype(f32) + begins[side] * came
        rank_side(0, m, side, normalize((scaled[i, 0], scaled[i, 1]), g))

    for d in range(SIDES):
        widths(d, TOUCH - 1, 1)

    def feature_copy(o):
        return rcopy(
            fsend.at[o], frecv.at[me], f_ss.at[o], f_rs.at[me],
            seq=lax.div(o, N_TP), tensor=lax.rem(o, N_TP))

    def place(j, _):
        o = lax.rem(me + 1 + j, GROUP)
        fsend[o] = placed(o, facc[o], (0,)).astype(bf16)

        @pl.when(j < GROUP - 1)
        def _():
            feature_copy(o).start()

        return 0

    lax.fori_loop(0, GROUP, place, 0)
    own_feature = pltpu.make_async_copy(fsend.at[me], frecv.at[me], f_ss.at[me])
    own_feature.start()

    lax.fori_loop(6, 8, main_tile, 0)

    def out_copy(i):
        rows = pl.ds(pl.multiple_of(i * TILE, TILE), TILE)
        return pltpu.make_async_copy(outv.at[rows, :], out_hbm.at[rows, :], out_sem.at[i])

    def fix(i, _):
        rows = pl.ds(pl.multiple_of(i * TILE, TILE), TILE)
        h = lax.div(i, 2)
        sub = pl.ds(pl.multiple_of(lax.rem(i, 2) * TILE, TILE), TILE)
        corr = lax.dot_general(low[h, 0, sub, :], ab[1], NT, preferred_element_type=f32)
        outv[rows, :] = (acc[rows, :] + SCALE * corr).astype(bf16)
        out_copy(i).start()
        return 0

    lax.fori_loop(0, BLK // TILE, fix, 0)

    def arrive(j, _):
        o = lax.rem(me + j, GROUP)
        rcopy(fsend.at[o], frecv.at[o], f_ss.at[o], f_rs.at[o],
              seq=lax.div(o, N_TP), tensor=lax.rem(o, N_TP)).wait_recv()
        return 0

    lax.fori_loop(1, GROUP, arrive, 0)

    for m in range(2):
        ex1(m).wait_send()
        ex2(m).wait_send()
        ex3(m, core).wait_send()
    mx(xh).wait_send()
    for a in range(2):
        for i in range(4):
            near_copy(a, i).wait_send()
            far_copy(a, i).wait_send()

    for d in range(SIDES):
        @pl.when(places[d] < N_SEQ - 1)
        def _():
            for c in range(CHUNKS):
                chain_copy(d, c).wait_send()

    def left(j, _):
        feature_copy(lax.rem(me + j, GROUP)).wait_send()
        return 0

    lax.fori_loop(1, GROUP, left, 0)
    own_feature.wait()
    for i in range(BLK // TILE):
        out_copy(i).wait()


def finish(att_in, feat_in, att_out, feat_out, buf, fbuf, fsum, in_sem, out_sem, f_in, f_out):
    def piece(i):
        return pl.ds(i * (BLK // PIECES), BLK // PIECES)

    def load(i):
        return pltpu.make_async_copy(att_in.at[piece(i), :], buf.at[piece(i), :], in_sem.at[i])

    def store(i):
        return pltpu.make_async_copy(buf.at[piece(i), :], att_out.at[piece(i), :], out_sem.at[i])

    features = pltpu.make_async_copy(feat_in, fbuf, f_in)
    features.start()
    for i in range(PIECES):
        load(i).start()
    for i in range(PIECES):
        load(i).wait()
        store(i).start()
    features.wait()

    def add(o, total):
        return total + fbuf[o].astype(f32)

    feat = lax.fori_loop(0, GROUP, add, jnp.zeros((2 * KR, KD), f32))
    fsum[pl.ds(0, 2 * KR, stride=2), :] = feat[:, :128]
    fsum[pl.ds(1, 2 * KR, stride=2), :] = feat[:, 128:]
    result = pltpu.make_async_copy(fsum, feat_out, f_out)
    result.start()
    result.wait()
    for i in range(PIECES):
        store(i).wait()


def per_device(x, g, a, b, w, m1, m2, r, q, bounds, owner):
    any_ = pl.BlockSpec(memory_space=pl.ANY)
    dma = pltpu.SemaphoreType.DMA
    V = pltpu.VMEM
    att, arrived = pl.pallas_call(
        kernel,
        out_shape=(
            jax.ShapeDtypeStruct((BLK, COLS), bf16),
            jax.ShapeDtypeStruct((GROUP, 2 * KR, KD), bf16),
        ),
        in_specs=[any_] * 11,
        out_specs=(any_, any_),
        scratch_shapes=[
            V((2, BLK, COLS), bf16), V((BLK, WIDTH), bf16), V((COLS, WIDTH), bf16),
            V((2, COLS, RANK), bf16), V((RANK, COLS), bf16), V((COLS, KD), bf16),
            V((2, 8, COLS), f32), V((2, 8, COLS), f32), V((KR, RANK), f32),
            pltpu.SMEM((2, EX), jnp.int32), pltpu.SMEM((1, EX), jnp.int32),
            V((BLK, COLS), f32), V((BLK, COLS), bf16),
            V((2, HALF, RANK), bf16), V((2, HALF, RANK), bf16), V((2, HALF, RANK), f32),
            V((2, HALF, RANK), bf16), V((2, HALF, RANK), bf16),
            V((2, 2, HALF, RANK), bf16), V((2 * RANK, BLK), bf16),
            V((2, TOUCH * RANK, COLS), bf16),
            V((SIDES, CHUNKS, SLICE, WIDE), bf16), V((SIDES, CHUNKS, SLICE, WIDE), bf16),
            V((N_Z, 2, 2, 16, COLS), bf16), V((4, 2, RANK, WIDE), f32),
            V((SIDES, TOUCH * 64, WIDE), bf16), V((SIDES, TOUCH, 2 * KR, KD), f32),
            V((GROUP, 2 * KR, KD), f32),
            V((GROUP, 2 * KR, KD), bf16),
            dma((24,)), dma((4,)), dma((3, 2)), dma((3, 2)), dma(()), dma(()),
            dma((2, 4)), dma((2, 4)), dma((2, 4)), dma((2, 4)), dma((SIDES, CHUNKS)), dma((SIDES, CHUNKS)),
            dma((GROUP,)), dma((GROUP,)),
        ],
        compiler_params=pltpu.CompilerParams(
            collective_id=0, has_side_effects=True, vmem_limit_bytes=VLIMIT * 2**20),
        name="step",
    )(
        x.reshape(BLK, COLS), g.reshape(BLK, WIDTH), a, b, w, m1, m2, r, q,
        bounds.reshape(2, EX), owner.reshape(1, EX),
    )
    att, feat = pl.pallas_call(
        finish,
        out_shape=(
            jax.ShapeDtypeStruct((BLK, COLS), bf16),
            jax.ShapeDtypeStruct((4 * KR, KD // 2), f32),
        ),
        in_specs=[any_, any_],
        out_specs=(any_, any_),
        scratch_shapes=[
            V((BLK, COLS), bf16), V((GROUP, 2 * KR, KD), bf16), V((4 * KR, KD // 2), f32),
            dma((PIECES,)), dma((PIECES,)), dma(()), dma(()),
        ],
        compiler_params=pltpu.CompilerParams(vmem_limit_bytes=VLIMIT * 2**20),
        name="finish",
    )(att, arrived)
    return att.reshape(1, BLK, COLS), feat.reshape(1, 1, 2 * KR * KD)


def solution(mesh):
    return jax.shard_map(
        per_device,
        mesh=mesh,
        in_specs=(
            P("dp", "seq", "tensor"),
            P("dp", "seq", None),
            P("tensor", None),
            P(None, "tensor"),
            P("tensor", None),
            P(None, "dp", "tensor"),
            P(None, "dp", "tensor"),
            P(),
            P(),
            P("dp", None, None),
            P("dp", None),
        ),
        out_specs=(P("dp", "seq", "tensor"), P("dp", ("seq", "tensor"), None)),
        check_vma=False,
    )
```

```python
import jax
import jax.numpy as jnp
from jax import lax
from jax.experimental import pallas as pl
from jax.experimental.pallas import tpu as pltpu
from jax.sharding import PartitionSpec as P

TOUCH = 8
SCALE = 4.0
BETA_ONE = 0.9
BETA_TWO = 0.999
EPSILON = 1e-08
SQUARE = (1.0 - BETA_TWO) / (1.0 - BETA_ONE) ** 2

N_DP, N_SEQ, N_TP = 16, 4, 4
GROUP = N_SEQ * N_TP
BLK = 1024
WIDTH = 4096
COLS = WIDTH // N_TP
RANK = 128
KR, KD = 16, 256
EX = 16
HALF = BLK // 2
TILE = 256
WIDE = 512
CHUNKS = 8
SLICE = 32
SIDES = 2
N_Z = 8
VLIMIT = 60
PIECES = 8

bf16 = jnp.bfloat16
f32 = jnp.float32
NT = (((1,), (1,)), ((), ()))
MESH_ID = pl.DeviceIdType.MESH


def kernel(
    x_hbm, g_hbm, a_hbm, b_hbm, w_hbm, m1_hbm, m2_hbm, r_hbm, q_hbm, bounds_hbm, owner_hbm,
    out_hbm, frecv,
    xg, gv, wv, ab, bv, qv, m1v, m2v, rv, bounds, owner, acc, outv,
    ex1s, ex1r, lowh, ex2s, ex2r, low, low_t, parts, cs, cr, mom, scaled, uv, fv, facc, fsend,
    ld_sem, out_sem, ex_ss, ex_rs, mx_ss, mx_rs, za_ss, za_rs, zb_ss, zb_rs, c_ss, c_rs, f_ss, f_rs,
):
    dp = lax.axis_index("dp")
    s = lax.axis_index("seq")
    t = lax.axis_index("tensor")
    core = lax.rem(t, 2)
    chip = lax.div(t, 2)
    partner = chip * 2 + (1 - core)
    across = (1 - chip) * 2 + core
    zi = lax.div(dp, 2)
    xh = lax.rem(dp, 2)
    xpeer = zi * 2 + (1 - xh)
    z_steps = (1, 2, N_Z - 1, N_Z - 2)
    z_peers = [lax.rem(zi + d, N_Z) * 2 + xh for d in z_steps]
    me = s * N_TP + t

    def col(i):
        return pl.ds(pl.multiple_of(lax.rem(t + i, N_TP) * COLS, COLS), COLS)

    def half_rows(h):
        return pl.ds(pl.multiple_of(h * HALF, HALF), HALF)

    def load(i, src, dst):
        return pltpu.make_async_copy(src, dst, ld_sem.at[i])

    ld_m1 = load(0, m1_hbm, m1v)
    ld_m2 = load(1, m2_hbm, m2v)
    ld_a = load(2, a_hbm, ab.at[1])
    ld_b = load(3, b_hbm, bv)
    ld_low = [
        load(4 + i, x_hbm.at[half_rows(h), :], xg.at[0, half_rows(h), :])
        for i, h in enumerate((1 - core, core))
    ] + [
        load(6 + i, g_hbm.at[half_rows(h), col(0)], xg.at[1, half_rows(h), :])
        for i, h in enumerate((1 - core, core))
    ]
    ld_g = [
        [load(8 + 4 * h + i, g_hbm.at[half_rows(h), col(i)], gv.at[half_rows(h), col(i)])
         for i in range(1, N_TP)] for h in range(2)
    ]
    own_g = [load(8 + 4 * h, xg.at[1, half_rows(h), :], gv.at[half_rows(h), col(0)])
             for h in range(2)]
    ld_w = [
        load(16 + i, w_hbm.at[pl.ds(i * TILE, TILE), :], wv.at[pl.ds(i * TILE, TILE), :])
        for i in range(4)
    ]
    ld_q = load(20, q_hbm.at[col(0), :], qv)
    ld_r = load(21, r_hbm, rv)
    ld_bounds = load(22, bounds_hbm, bounds)
    ld_owner = load(23, owner_hbm, owner)
    for c in (ld_m1, ld_m2, ld_a, ld_low[0], ld_low[1], ld_b, ld_low[2], ld_low[3], *ld_g[0],
              ld_w[0], *ld_g[1], *ld_w[1:], ld_q, ld_r, ld_bounds, ld_owner):
        c.start()

    barrier = pltpu.get_barrier_semaphore()

    def greet(j, _):
        o = lax.rem(me + j, GROUP)
        pl.semaphore_signal(
            barrier, inc=1, device_id={"seq": lax.div(o, N_TP), "tensor": lax.rem(o, N_TP)},
            device_id_type=MESH_ID)
        return 0

    lax.fori_loop(1, GROUP, greet, 0)
    for peer in (xpeer, *z_peers):
        pl.semaphore_signal(barrier, inc=1, device_id={"dp": peer}, device_id_type=MESH_ID)

    def rcopy(src, dst, ss, rs, **where):
        return pltpu.make_async_remote_copy(
            src_ref=src, dst_ref=dst, send_sem=ss, recv_sem=rs, device_id=where,
            device_id_type=MESH_ID)

    def ex1(m):
        return rcopy(ex1s.at[m], ex1r.at[m], ex_ss.at[0, m], ex_rs.at[0, m], tensor=partner)

    def ex2(m):
        return rcopy(ex2s.at[m], ex2r.at[m], ex_ss.at[1, m], ex_rs.at[1, m], tensor=across)

    def ex3(m, half):
        return rcopy(low.at[half, m], low.at[half, m], ex_ss.at[2, m], ex_rs.at[2, m],
                     tensor=partner)

    def second(m):
        ex1(m).wait_recv()
        total = lowh[m] + ex1r[m].astype(f32)
        lowh[m] = total
        ex2s[m] = total.astype(bf16)
        ex2(m).start()

    def third(m):
        ex2(m).wait_recv()
        low[core, m] = (lowh[m] + ex2r[m].astype(f32)).astype(bf16)
        ex3(m, core).start()

    sides_x = (xh, 1 - xh)

    def mx(x):
        return rcopy(mom.at[zi, xh], mom.at[zi, x], mx_ss, mx_rs, dp=xpeer)

    def near_copy(a, i):
        block = mom.at[zi, sides_x[a]]
        return rcopy(block, block, za_ss.at[a, i], za_rs.at[a, i], dp=z_peers[i])

    def near_wait(a, i):
        block = mom.at[lax.rem(zi + N_Z - z_steps[i], N_Z), sides_x[a]]
        rcopy(block, block, za_ss.at[a, i], za_rs.at[a, i], dp=z_peers[i]).wait_recv()

    def far_block(a, i, hops):
        d = z_steps[i] if i < 2 else z_steps[i] - N_Z
        side = 1 if d > 0 else -1
        z = lax.rem(zi + 2 * N_Z - side * hops, N_Z)
        x = sides_x[a]
        if d in (1, -1):
            return mom.at[z, x]
        return mom.at[z, x, 0 if d > 0 else 1]

    def far_copy(a, i):
        block = far_block(a, i, 2)
        return rcopy(block, block, zb_ss.at[a, i], zb_rs.at[a, i], dp=z_peers[i])

    def far_wait(a, i):
        block = far_block(a, i, 3 + i % 2)
        rcopy(block, block, zb_ss.at[a, i], zb_rs.at[a, i], dp=z_peers[i]).wait_recv()

    def round_one(a):
        if a == 1:
            mx(1 - xh).wait_recv()
        for i in (1, 3, 0, 2):
            near_copy(a, i).start()

    def round_two(a):
        for i in (1, 3):
            near_wait(a, i)
        for i in range(4):
            far_copy(a, i).start()

    ld_b.wait()
    ab[0] = bv[...].T
    ld_m1.wait()
    ld_m2.wait()
    for mm in range(2):
        mom[zi, xh, mm] = jnp.concatenate([m1v[mm], m2v[mm]], axis=0).astype(bf16)
    ld_a.wait()

    def partial(i, _):
        m = 1 - lax.div(i, 2)
        late = lax.rem(i, 2)
        rows = half_rows(jnp.where(late == 1, core, 1 - core))

        for n in range(4):
            @pl.when(i == n)
            def _():
                ld_low[n].wait()

        p = jnp.dot(xg[1 - m, rows, :], ab[m], preferred_element_type=f32)

        @pl.when(late == 0)
        def _():
            ex1s[m] = p.astype(bf16)

        @pl.when(late == 1)
        def _():
            lowh[m] = p

        @pl.when(i == 1)
        def _():
            pl.semaphore_wait(barrier, GROUP - 1 + 5)
            ex1(1).start()
            mx(xh).start()
            round_one(0)

        @pl.when(i == 2)
        def _():
            ex1(0).start()

        return 0

    lax.fori_loop(0, 4, partial, 0)
    for c in own_g:
        c.start()
    second(1)

    for c in ld_g[0]:
        c.wait()
    own_g[0].wait()
    ld_w[0].wait()
    second(0)

    ld_bounds.wait()
    ld_owner.wait()
    low_pos = s * BLK
    n_le = jnp.int32(0)
    n_lt = jnp.int32(0)
    n_last = jnp.int32(0)
    n_next = jnp.int32(0)
    pos = low_pos + lax.broadcasted_iota(jnp.int32, (1, BLK), 1)
    ids = jnp.full((1, BLK), -1, jnp.int32)
    for e in range(EX):
        st = bounds[0, e]
        n_le = n_le + (st <= low_pos).astype(jnp.int32)
        n_lt = n_lt + (st < low_pos).astype(jnp.int32)
        n_last = n_last + (st <= low_pos + BLK - 1).astype(jnp.int32)
        n_next = n_next + (st <= low_pos + BLK).astype(jnp.int32)
        ids = ids + (st <= pos).astype(jnp.int32)
    first_id = n_le - 1
    last_id = n_last - 1
    n_slots = last_id - first_id
    single = (first_id == last_id).astype(f32)
    inside = (s < N_SEQ - 1).astype(jnp.int32)
    from_left = (n_le == n_lt).astype(f32)
    from_right = ((n_next == n_last).astype(jnp.int32) * inside).astype(f32)
    begins = (from_left, from_right)
    keeps = (from_left * single, from_right * single)

    def mask_of(side, k):
        slot = jnp.where(side == 0, ids - first_id, last_id - ids)
        return (slot == k).astype(f32).astype(bf16)

    def rank_rows(m):
        return pl.ds(pl.multiple_of(m * RANK, RANK), RANK)

    places = (s, N_SEQ - 1 - s)
    nexts = (lax.rem(s + 1, N_SEQ), lax.rem(s + N_SEQ - 1, N_SEQ))

    def chain_copy(d, c):
        return rcopy(cs.at[d, c], cr.at[d, c], c_ss.at[d, c], c_rs.at[d, c], seq=nexts[d])

    def chain(place, c):
        for d in range(SIDES):
            @pl.when(places[d] == place)
            def _():
                if place > 0:
                    chain_copy(d, c).wait_recv()
                    cs[d, c] = (
                        cs[d, c].astype(f32) + keeps[d] * cr[d, c].astype(f32)).astype(bf16)
                chain_copy(d, c).start()

    def far(m):
        ex3(m, 1 - core).wait_recv()
        for h in range(2):
            low_t[m * RANK:(m + 1) * RANK, h * HALF:(h + 1) * HALF] = (
                low[h, m].astype(f32) * SCALE).T.astype(bf16)

        def one(side, _):
            left = low_t[m * RANK:(m + 1) * RANK, :] * mask_of(side, n_slots)
            p = jnp.dot(left, xg[m, :, half_rows(side)], preferred_element_type=f32).astype(bf16)
            for c in range(CHUNKS // 2):
                cs[side, (1 - m) * (CHUNKS // 2) + c] = p[c * SLICE:(c + 1) * SLICE]
            return 0

        lax.fori_loop(0, SIDES, one, 0)
        for c in range(CHUNKS // 2):
            chain(0, (1 - m) * (CHUNKS // 2) + c)

    def main_tile(i, _):
        @pl.when(i == 1)
        def _():
            for c in ld_g[1]:
                c.wait()
            own_g[1].wait()

        for n in (1, 2, 3):
            @pl.when(i == 2 * n)
            def _():
                ld_w[n].wait()

        @pl.when(i == 2)
        def _():
            round_one(1)

        @pl.when(i == 4)
        def _():
            third(1)

        @pl.when(i == 5)
        def _():
            far(1)
            third(0)
            round_two(0)

        rows = half_rows(lax.rem(i, 2))
        cc = pl.ds(pl.multiple_of(lax.div(i, 2) * TILE, TILE), TILE)
        acc[rows, cc] = lax.dot_general(
            gv[rows, :], wv[cc, :], NT, preferred_element_type=f32)
        return 0

    lax.fori_loop(0, 6, main_tile, 0)

    far(0)

    @pl.when(s == 0)
    def _():
        cr[0] = jnp.zeros((CHUNKS, SLICE, WIDE), bf16)

    @pl.when(s == N_SEQ - 1)
    def _():
        cr[1] = jnp.zeros((CHUNKS, SLICE, WIDE), bf16)

    def part_tile(i, _):
        m = lax.div(i, 4)
        side = lax.rem(lax.div(i, 2), 2)
        group = lax.rem(i, 2)

        for n, steps in (
            (1, ((1, 0),)), (2, ((1, 1),)), (3, ((1, 2),)), (4, ((1, 3),)),
            (5, ((1, 4), (2, 0))), (6, ((1, 5), (2, 1))), (7, ((1, 6), (2, 2))),
        ):
            @pl.when(i == n)
            def _():
                for place, c in steps:
                    chain(place, c)

        @pl.when(i == 0)
        def _():
            round_two(1)

        low_m = low_t[rank_rows(m), :]
        left = jnp.concatenate([low_m * mask_of(side, group * 4 + k) for k in range(4)], axis=0)
        p = jnp.dot(left, xg[m, :, half_rows(side)], preferred_element_type=f32)
        parts[m, half_rows(group), half_rows(side)] = (p * (1.0 - BETA_ONE)).astype(bf16)
        return 0

    lax.fori_loop(0, 8, part_tile, 0)
    chain(1, 7)
    chain(2, 3)

    for a in range(2):
        for i in (0, 2):
            near_wait(a, i)
        for i in range(4):
            far_wait(a, i)
    ld_q.wait()
    ld_r.wait()
    r = rv[...]
    r_hi = r.astype(bf16)
    r_lo = (r - r_hi.astype(f32)).astype(bf16)
    r2 = jnp.concatenate([r_hi, r_lo], axis=0)

    go = []
    for k in range(TOUCH):
        e = jnp.minimum(first_id + k, EX - 1)
        done = (k <= n_slots) & (bounds[1, e] <= low_pos + BLK)
        left_go = jnp.where(done, owner[0, e], -1)
        e = jnp.maximum(last_id - k, 0)
        done = (k <= n_slots) & (bounds[0, e] >= low_pos)
        go.append((left_go, jnp.where(done, owner[0, e], -1)))

    def widths(side, lo, n):
        u = uv[side, lo * 64:(lo + n) * 64, :]
        f = jnp.dot(u, qv[side * WIDE:(side + 1) * WIDE, :], preferred_element_type=f32)
        for i in range(n):
            v = f[i * 64:(i + 1) * 64]
            fv[side, lo + i] = jnp.concatenate(
                [v[:KR] + v[KR:2 * KR], v[2 * KR:3 * KR] + v[3 * KR:]], axis=0)

    def placed(o, total, slots):
        for k in slots:
            for d in range(SIDES):
                total = total + jnp.where(go[k][d] == o, 1.0, 0.0) * fv[d, (k + TOUCH - 1) % TOUCH]
        return total

    def moments_of(m, z, cc):
        a = mom[z, 0, m, :, cc].astype(f32)
        b = mom[z, 1, m, :, cc].astype(f32)
        return (
            BETA_ONE * jnp.concatenate([a[:8], b[:8]], axis=0),
            BETA_TWO * jnp.concatenate([a[8:], b[8:]], axis=0),
        )

    def normalize(scaled, g):
        first = scaled[0] + g
        second = scaled[1] + SQUARE * (g * g)
        root = second * lax.rsqrt(second) + EPSILON
        return (first * lax.rsqrt(root * root)).astype(bf16)

    def rank_side(k, m, side, n):
        row = (k + TOUCH - 1) % TOUCH * 64 + m * 32
        u = jnp.dot(r2, n, preferred_element_type=f32)
        u = u[:KR] + u[KR:]
        hi = u.astype(bf16)
        if not isinstance(row, int):
            row = pl.multiple_of(row, 32)
        uv[side, pl.ds(row, 16), :] = hi
        uv[side, pl.ds(row + 16, 16), :] = (u - hi.astype(f32)).astype(bf16)

    def scale_moments(m, side):
        cc = half_rows(side)
        for z in range(N_Z):
            for i, v in enumerate(moments_of(m, z, cc)):
                scaled[2 * side + m, i, z * 16:z * 16 + 16, :] = v

    def seven(i, _):
        m = lax.rem(i, 2)
        side = lax.div(i, 2)
        for n, steps in (
            (0, ((2, 4),)), (1, ((2, 5),)), (2, ((2, 6), (2, 7))),
        ):
            @pl.when(i == n)
            def _():
                for place, c in steps:
                    chain(place, c)

        scale_moments(m, side)
        for k in range(1, TOUCH):
            g = parts[m, k * RANK:(k + 1) * RANK, half_rows(side)].astype(f32)
            rank_side(k, m, side, normalize((scaled[i, 0], scaled[i, 1]), g))
        return 0

    lax.fori_loop(0, 4, seven, 0)

    for d in range(SIDES):
        widths(d, 0, TOUCH - 1)

    def place_most(o, _):
        facc[o] = placed(o, jnp.zeros((2 * KR, KD), f32), range(1, TOUCH))
        return 0

    lax.fori_loop(0, GROUP, place_most, 0)

    for d in range(SIDES):
        @pl.when(places[d] == N_SEQ - 1)
        def _():
            for c in range(CHUNKS):
                chain_copy(d, c).wait_recv()

    for i in range(4):
        m = i % 2
        side = i // 2
        came = jnp.concatenate(
            [cr[side, (1 - m) * (CHUNKS // 2) + c].astype(f32) for c in range(CHUNKS // 2)], axis=0)
        g = parts[m, :RANK, side * WIDE:(side + 1) * WIDE].astype(f32) + begins[side] * (1.0 - BETA_ONE) * came
        rank_side(0, m, side, normalize((scaled[i, 0], scaled[i, 1]), g))

    for d in range(SIDES):
        widths(d, TOUCH - 1, 1)

    def feature_copy(o):
        return rcopy(
            fsend.at[o], frecv.at[me], f_ss.at[o], f_rs.at[me],
            seq=lax.div(o, N_TP), tensor=lax.rem(o, N_TP))

    def place(j, _):
        o = lax.rem(me + 1 + j, GROUP)
        fsend[o] = placed(o, facc[o], (0,)).astype(bf16)

        @pl.when(j < GROUP - 1)
        def _():
            feature_copy(o).start()

        return 0

    lax.fori_loop(0, GROUP, place, 0)
    own_feature = pltpu.make_async_copy(fsend.at[me], frecv.at[me], f_ss.at[me])
    own_feature.start()

    lax.fori_loop(6, 8, main_tile, 0)

    def out_copy(i):
        rows = pl.ds(pl.multiple_of(i * TILE, TILE), TILE)
        return pltpu.make_async_copy(outv.at[rows, :], out_hbm.at[rows, :], out_sem.at[i])

    def fix(i, _):
        rows = pl.ds(pl.multiple_of(i * TILE, TILE), TILE)
        h = lax.div(i, 2)
        sub = pl.ds(pl.multiple_of(lax.rem(i, 2) * TILE, TILE), TILE)
        corr = lax.dot_general(low[h, 0, sub, :], ab[1], NT, preferred_element_type=f32)
        outv[rows, :] = (acc[rows, :] + SCALE * corr).astype(bf16)
        out_copy(i).start()
        return 0

    lax.fori_loop(0, BLK // TILE, fix, 0)

    def arrive(j, _):
        o = lax.rem(me + j, GROUP)
        rcopy(fsend.at[o], frecv.at[o], f_ss.at[o], f_rs.at[o],
              seq=lax.div(o, N_TP), tensor=lax.rem(o, N_TP)).wait_recv()
        return 0

    lax.fori_loop(1, GROUP, arrive, 0)

    for m in range(2):
        ex1(m).wait_send()
        ex2(m).wait_send()
        ex3(m, core).wait_send()
    mx(xh).wait_send()
    for a in range(2):
        for i in range(4):
            near_copy(a, i).wait_send()
            far_copy(a, i).wait_send()

    for d in range(SIDES):
        @pl.when(places[d] < N_SEQ - 1)
        def _():
            for c in range(CHUNKS):
                chain_copy(d, c).wait_send()

    def left(j, _):
        feature_copy(lax.rem(me + j, GROUP)).wait_send()
        return 0

    lax.fori_loop(1, GROUP, left, 0)
    own_feature.wait()
    for i in range(BLK // TILE):
        out_copy(i).wait()


def finish(att_in, feat_in, att_out, feat_out, buf, fbuf, fsum, in_sem, out_sem, f_in, f_out):
    def piece(i):
        return pl.ds(i * (BLK // PIECES), BLK // PIECES)

    def load(i):
        return pltpu.make_async_copy(att_in.at[piece(i), :], buf.at[piece(i), :], in_sem.at[i])

    def store(i):
        return pltpu.make_async_copy(buf.at[piece(i), :], att_out.at[piece(i), :], out_sem.at[i])

    features = pltpu.make_async_copy(feat_in, fbuf, f_in)
    features.start()
    for i in range(PIECES):
        load(i).start()
    for i in range(PIECES):
        load(i).wait()
        store(i).start()
    features.wait()

    def add(o, total):
        return total + fbuf[o].astype(f32)

    feat = lax.fori_loop(0, GROUP, add, jnp.zeros((2 * KR, KD), f32))
    fsum[pl.ds(0, 2 * KR, stride=2), :] = feat[:, :128]
    fsum[pl.ds(1, 2 * KR, stride=2), :] = feat[:, 128:]
    result = pltpu.make_async_copy(fsum, feat_out, f_out)
    result.start()
    result.wait()
    for i in range(PIECES):
        store(i).wait()


def per_device(x, g, a, b, w, m1, m2, r, q, bounds, owner):
    any_ = pl.BlockSpec(memory_space=pl.ANY)
    dma = pltpu.SemaphoreType.DMA
    V = pltpu.VMEM
    att, arrived = pl.pallas_call(
        kernel,
        out_shape=(
            jax.ShapeDtypeStruct((BLK, COLS), bf16),
            jax.ShapeDtypeStruct((GROUP, 2 * KR, KD), bf16),
        ),
        in_specs=[any_] * 11,
        out_specs=(any_, any_),
        scratch_shapes=[
            V((2, BLK, COLS), bf16), V((BLK, WIDTH), bf16), V((COLS, WIDTH), bf16),
            V((2, COLS, RANK), bf16), V((RANK, COLS), bf16), V((COLS, KD), bf16),
            V((2, 8, COLS), f32), V((2, 8, COLS), f32), V((KR, RANK), f32),
            pltpu.SMEM((2, EX), jnp.int32), pltpu.SMEM((1, EX), jnp.int32),
            V((BLK, COLS), f32), V((BLK, COLS), bf16),
            V((2, HALF, RANK), bf16), V((2, HALF, RANK), bf16), V((2, HALF, RANK), f32),
            V((2, HALF, RANK), bf16), V((2, HALF, RANK), bf16),
            V((2, 2, HALF, RANK), bf16), V((2 * RANK, BLK), bf16),
            V((2, TOUCH * RANK, COLS), bf16),
            V((SIDES, CHUNKS, SLICE, WIDE), bf16), V((SIDES, CHUNKS, SLICE, WIDE), bf16),
            V((N_Z, 2, 2, 16, COLS), bf16), V((4, 2, RANK, WIDE), f32),
            V((SIDES, TOUCH * 64, WIDE), bf16), V((SIDES, TOUCH, 2 * KR, KD), f32),
            V((GROUP, 2 * KR, KD), f32),
            V((GROUP, 2 * KR, KD), bf16),
            dma((24,)), dma((4,)), dma((3, 2)), dma((3, 2)), dma(()), dma(()),
            dma((2, 4)), dma((2, 4)), dma((2, 4)), dma((2, 4)), dma((SIDES, CHUNKS)), dma((SIDES, CHUNKS)),
            dma((GROUP,)), dma((GROUP,)),
        ],
        compiler_params=pltpu.CompilerParams(
            collective_id=0, has_side_effects=True, vmem_limit_bytes=VLIMIT * 2**20),
        name="step",
    )(
        x.reshape(BLK, COLS), g.reshape(BLK, WIDTH), a, b, w, m1, m2, r, q,
        bounds.reshape(2, EX), owner.reshape(1, EX),
    )
    att, feat = pl.pallas_call(
        finish,
        out_shape=(
            jax.ShapeDtypeStruct((BLK, COLS), bf16),
            jax.ShapeDtypeStruct((4 * KR, KD // 2), f32),
        ),
        in_specs=[any_, any_],
        out_specs=(any_, any_),
        scratch_shapes=[
            V((BLK, COLS), bf16), V((GROUP, 2 * KR, KD), bf16), V((4 * KR, KD // 2), f32),
            dma((PIECES,)), dma((PIECES,)), dma(()), dma(()),
        ],
        compiler_params=pltpu.CompilerParams(vmem_limit_bytes=VLIMIT * 2**20),
        name="finish",
    )(att, arrived)
    return att.reshape(1, BLK, COLS), feat.reshape(1, 1, 2 * KR * KD)


def solution(mesh):
    return jax.shard_map(
        per_device,
        mesh=mesh,
        in_specs=(
            P("dp", "seq", "tensor"),
            P("dp", "seq", None),
            P("tensor", None),
            P(None, "tensor"),
            P("tensor", None),
            P(None, "dp", "tensor"),
            P(None, "dp", "tensor"),
            P(),
            P(),
            P("dp", None, None),
            P("dp", None),
        ),
        out_specs=(P("dp", "seq", "tensor"), P("dp", ("seq", "tensor"), None)),
        check_vma=False,
    )
```

```python
import jax
import jax.numpy as jnp
from jax import lax
from jax.experimental import pallas as pl
from jax.experimental.pallas import tpu as pltpu
from jax.sharding import PartitionSpec as P

TOUCH = 8
SCALE = 4.0
BETA_ONE = 0.9
BETA_TWO = 0.999
EPSILON = 1e-08
SQUARE = (1.0 - BETA_TWO) / (1.0 - BETA_ONE) ** 2

N_DP, N_SEQ, N_TP = 16, 4, 4
GROUP = N_SEQ * N_TP
BLK = 1024
WIDTH = 4096
COLS = WIDTH // N_TP
RANK = 128
KR, KD = 16, 256
EX = 16
HALF = BLK // 2
TILE = 256
WIDE = 512
CHUNKS = 8
SLICE = 32
SIDES = 2
N_Z = 8
VLIMIT = 60
PIECES = 8

bf16 = jnp.bfloat16
f32 = jnp.float32
NT = (((1,), (1,)), ((), ()))
MESH_ID = pl.DeviceIdType.MESH


def kernel(
    x_hbm, g_hbm, a_hbm, b_hbm, w_hbm, m1_hbm, m2_hbm, r_hbm, q_hbm, bounds_hbm, owner_hbm,
    out_hbm, frecv,
    xg, gv, wv, ab, bv, qv, m1v, m2v, rv, bounds, owner, acc, outv,
    ex1s, ex1r, lowh, ex2s, ex2r, low, low_t, parts, cs, cr, mom, scaled, uv, fv, facc, fsend,
    ld_sem, out_sem, ex_ss, ex_rs, mx_ss, mx_rs, za_ss, za_rs, zb_ss, zb_rs, c_ss, c_rs, f_ss, f_rs,
):
    dp = lax.axis_index("dp")
    s = lax.axis_index("seq")
    t = lax.axis_index("tensor")
    core = lax.rem(t, 2)
    chip = lax.div(t, 2)
    partner = chip * 2 + (1 - core)
    across = (1 - chip) * 2 + core
    zi = lax.div(dp, 2)
    xh = lax.rem(dp, 2)
    xpeer = zi * 2 + (1 - xh)
    z_steps = (1, 2, N_Z - 1, N_Z - 2)
    z_peers = [lax.rem(zi + d, N_Z) * 2 + xh for d in z_steps]
    me = s * N_TP + t

    def col(i):
        return pl.ds(pl.multiple_of(lax.rem(t + i, N_TP) * COLS, COLS), COLS)

    def half_rows(h):
        return pl.ds(pl.multiple_of(h * HALF, HALF), HALF)

    def load(i, src, dst):
        return pltpu.make_async_copy(src, dst, ld_sem.at[i])

    ld_m1 = load(0, m1_hbm, m1v)
    ld_m2 = load(1, m2_hbm, m2v)
    ld_a = load(2, a_hbm, ab.at[1])
    ld_b = load(3, b_hbm, bv)
    ld_low = [
        load(4 + i, x_hbm.at[half_rows(h), :], xg.at[0, half_rows(h), :])
        for i, h in enumerate((1 - core, core))
    ] + [
        load(6 + i, g_hbm.at[half_rows(h), col(0)], xg.at[1, half_rows(h), :])
        for i, h in enumerate((1 - core, core))
    ]
    ld_g = [
        [load(8 + 4 * h + i, g_hbm.at[half_rows(h), col(i)], gv.at[half_rows(h), col(i)])
         for i in range(1, N_TP)] for h in range(2)
    ]
    own_g = [load(8 + 4 * h, xg.at[1, half_rows(h), :], gv.at[half_rows(h), col(0)])
             for h in range(2)]
    ld_w = [
        load(16 + i, w_hbm.at[pl.ds(i * TILE, TILE), :], wv.at[pl.ds(i * TILE, TILE), :])
        for i in range(4)
    ]
    ld_q = load(20, q_hbm.at[col(0), :], qv)
    ld_r = load(21, r_hbm, rv)
    ld_bounds = load(22, bounds_hbm, bounds)
    ld_owner = load(23, owner_hbm, owner)
    for c in (ld_m1, ld_m2, ld_a, ld_low[0], ld_low[1], ld_b, ld_low[2], ld_low[3], *ld_g[0],
              ld_w[0], *ld_g[1], *ld_w[1:], ld_q, ld_r, ld_bounds, ld_owner):
        c.start()

    barrier = pltpu.get_barrier_semaphore()

    def greet(j, _):
        o = lax.rem(me + j, GROUP)
        pl.semaphore_signal(
            barrier, inc=1, device_id={"seq": lax.div(o, N_TP), "tensor": lax.rem(o, N_TP)},
            device_id_type=MESH_ID)
        return 0

    lax.fori_loop(1, GROUP, greet, 0)
    for peer in (xpeer, *z_peers):
        pl.semaphore_signal(barrier, inc=1, device_id={"dp": peer}, device_id_type=MESH_ID)

    def rcopy(src, dst, ss, rs, **where):
        return pltpu.make_async_remote_copy(
            src_ref=src, dst_ref=dst, send_sem=ss, recv_sem=rs, device_id=where,
            device_id_type=MESH_ID)

    def ex1(m):
        return rcopy(ex1s.at[m], ex1r.at[m], ex_ss.at[0, m], ex_rs.at[0, m], tensor=partner)

    def ex2(m):
        return rcopy(ex2s.at[m], ex2r.at[m], ex_ss.at[1, m], ex_rs.at[1, m], tensor=across)

    def ex3(m, half):
        return rcopy(low.at[half, m], low.at[half, m], ex_ss.at[2, m], ex_rs.at[2, m],
                     tensor=partner)

    def second(m):
        ex1(m).wait_recv()
        total = lowh[m] + ex1r[m].astype(f32)
        lowh[m] = total
        ex2s[m] = total.astype(bf16)
        ex2(m).start()

    def third(m):
        ex2(m).wait_recv()
        low[core, m] = (lowh[m] + ex2r[m].astype(f32)).astype(bf16)
        ex3(m, core).start()

    sides_x = (xh, 1 - xh)

    def mx(x):
        return rcopy(mom.at[zi, xh], mom.at[zi, x], mx_ss, mx_rs, dp=xpeer)

    def near_copy(a, i):
        block = mom.at[zi, sides_x[a]]
        return rcopy(block, block, za_ss.at[a, i], za_rs.at[a, i], dp=z_peers[i])

    def near_wait(a, i):
        block = mom.at[lax.rem(zi + N_Z - z_steps[i], N_Z), sides_x[a]]
        rcopy(block, block, za_ss.at[a, i], za_rs.at[a, i], dp=z_peers[i]).wait_recv()

    def far_block(a, i, hops):
        d = z_steps[i] if i < 2 else z_steps[i] - N_Z
        side = 1 if d > 0 else -1
        z = lax.rem(zi + 2 * N_Z - side * hops, N_Z)
        x = sides_x[a]
        if d in (1, -1):
            return mom.at[z, x]
        return mom.at[z, x, 0 if d > 0 else 1]

    def far_copy(a, i):
        block = far_block(a, i, 2)
        return rcopy(block, block, zb_ss.at[a, i], zb_rs.at[a, i], dp=z_peers[i])

    def far_wait(a, i):
        block = far_block(a, i, 3 + i % 2)
        rcopy(block, block, zb_ss.at[a, i], zb_rs.at[a, i], dp=z_peers[i]).wait_recv()

    def round_one(a):
        if a == 1:
            mx(1 - xh).wait_recv()
        for i in (1, 3, 0, 2):
            near_copy(a, i).start()

    def round_two(a):
        for i in (1, 3):
            near_wait(a, i)
        for i in range(4):
            far_copy(a, i).start()

    ld_b.wait()
    ab[0] = bv[...].T
    ld_m1.wait()
    ld_m2.wait()
    for mm in range(2):
        mom[zi, xh, mm] = jnp.concatenate([m1v[mm], m2v[mm]], axis=0).astype(bf16)
    ld_a.wait()

    def partial(i, _):
        m = 1 - lax.div(i, 2)
        late = lax.rem(i, 2)
        rows = half_rows(jnp.where(late == 1, core, 1 - core))

        for n in range(4):
            @pl.when(i == n)
            def _():
                ld_low[n].wait()

        p = jnp.dot(xg[1 - m, rows, :], ab[m], preferred_element_type=f32)

        @pl.when(late == 0)
        def _():
            ex1s[m] = p.astype(bf16)

        @pl.when(late == 1)
        def _():
            lowh[m] = p

        @pl.when(i == 1)
        def _():
            pl.semaphore_wait(barrier, GROUP - 1 + 5)
            ex1(1).start()
            mx(xh).start()
            round_one(0)

        @pl.when(i == 2)
        def _():
            ex1(0).start()

        return 0

    lax.fori_loop(0, 4, partial, 0)
    for c in own_g:
        c.start()
    second(1)

    for c in ld_g[0]:
        c.wait()
    own_g[0].wait()
    ld_w[0].wait()
    second(0)

    ld_bounds.wait()
    ld_owner.wait()
    low_pos = s * BLK
    n_le = jnp.int32(0)
    n_lt = jnp.int32(0)
    n_last = jnp.int32(0)
    n_next = jnp.int32(0)
    pos = low_pos + lax.broadcasted_iota(jnp.int32, (1, BLK), 1)
    ids = jnp.full((1, BLK), -1, jnp.int32)
    for e in range(EX):
        st = bounds[0, e]
        n_le = n_le + (st <= low_pos).astype(jnp.int32)
        n_lt = n_lt + (st < low_pos).astype(jnp.int32)
        n_last = n_last + (st <= low_pos + BLK - 1).astype(jnp.int32)
        n_next = n_next + (st <= low_pos + BLK).astype(jnp.int32)
        ids = ids + (st <= pos).astype(jnp.int32)
    first_id = n_le - 1
    last_id = n_last - 1
    n_slots = last_id - first_id
    single = (first_id == last_id).astype(f32)
    inside = (s < N_SEQ - 1).astype(jnp.int32)
    from_left = (n_le == n_lt).astype(f32)
    from_right = ((n_next == n_last).astype(jnp.int32) * inside).astype(f32)
    begins = (from_left, from_right)
    keeps = (from_left * single, from_right * single)

    def mask_of(side, k):
        slot = jnp.where(side == 0, ids - first_id, last_id - ids)
        return (slot == k).astype(f32).astype(bf16)

    def rank_rows(m):
        return pl.ds(pl.multiple_of(m * RANK, RANK), RANK)

    places = (s, N_SEQ - 1 - s)
    nexts = (lax.rem(s + 1, N_SEQ), lax.rem(s + N_SEQ - 1, N_SEQ))

    def chain_copy(d, c):
        return rcopy(cs.at[d, c], cr.at[d, c], c_ss.at[d, c], c_rs.at[d, c], seq=nexts[d])

    def chain(place, c):
        for d in range(SIDES):
            @pl.when(places[d] == place)
            def _():
                if place > 0:
                    chain_copy(d, c).wait_recv()
                    cs[d, c] = (
                        cs[d, c].astype(f32) + keeps[d] * cr[d, c].astype(f32)).astype(bf16)
                chain_copy(d, c).start()

    def far(m):
        ex3(m, 1 - core).wait_recv()
        for h in range(2):
            low_t[m * RANK:(m + 1) * RANK, h * HALF:(h + 1) * HALF] = (
                low[h, m].astype(f32) * SCALE).T.astype(bf16)

        def one(side, _):
            left = low_t[m * RANK:(m + 1) * RANK, :] * mask_of(side, n_slots)
            p = jnp.dot(left, xg[m, :, half_rows(side)], preferred_element_type=f32).astype(bf16)
            for c in range(CHUNKS // 2):
                cs[side, (1 - m) * (CHUNKS // 2) + c] = p[c * SLICE:(c + 1) * SLICE]
            return 0

        lax.fori_loop(0, SIDES, one, 0)
        for c in range(CHUNKS // 2):
            chain(0, (1 - m) * (CHUNKS // 2) + c)

    def main_tile(i, _):
        @pl.when(i == 1)
        def _():
            for c in ld_g[1]:
                c.wait()
            own_g[1].wait()

        for n in (1, 2, 3):
            @pl.when(i == 2 * n)
            def _():
                ld_w[n].wait()

        @pl.when(i == 2)
        def _():
            round_one(1)

        @pl.when(i == 4)
        def _():
            third(1)

        @pl.when(i == 5)
        def _():
            far(1)
            third(0)
            round_two(0)

        rows = half_rows(lax.rem(i, 2))
        cc = pl.ds(pl.multiple_of(lax.div(i, 2) * TILE, TILE), TILE)
        acc[rows, cc] = lax.dot_general(
            gv[rows, :], wv[cc, :], NT, preferred_element_type=f32)
        return 0

    lax.fori_loop(0, 6, main_tile, 0)

    far(0)

    @pl.when(s == 0)
    def _():
        cr[0] = jnp.zeros((CHUNKS, SLICE, WIDE), bf16)

    @pl.when(s == N_SEQ - 1)
    def _():
        cr[1] = jnp.zeros((CHUNKS, SLICE, WIDE), bf16)

    def part_tile(i, _):
        m = lax.div(i, 4)
        side = lax.rem(lax.div(i, 2), 2)
        group = lax.rem(i, 2)

        for n, steps in (
            (1, ((1, 0),)), (2, ((1, 1),)), (3, ((1, 2),)), (4, ((1, 3),)),
            (5, ((1, 4), (2, 0))), (6, ((1, 5), (2, 1))), (7, ((1, 6), (2, 2))),
        ):
            @pl.when(i == n)
            def _():
                for place, c in steps:
                    chain(place, c)

        @pl.when(i == 0)
        def _():
            round_two(1)

        low_m = low_t[rank_rows(m), :]
        left = jnp.concatenate([low_m * mask_of(side, group * 4 + k) for k in range(4)], axis=0)
        p = jnp.dot(left, xg[m, :, half_rows(side)], preferred_element_type=f32)
        parts[m, half_rows(group), half_rows(side)] = (p * (1.0 - BETA_ONE)).astype(bf16)
        return 0

    lax.fori_loop(0, 8, part_tile, 0)
    chain(1, 7)
    chain(2, 3)

    for a in range(2):
        for i in (0, 2):
            near_wait(a, i)
        for i in range(4):
            far_wait(a, i)
    ld_q.wait()
    ld_r.wait()
    r = rv[...]
    r_hi = r.astype(bf16)
    r_lo = (r - r_hi.astype(f32)).astype(bf16)
    r2 = jnp.concatenate([r_hi, r_lo], axis=0)

    go = []
    for k in range(TOUCH):
        e = jnp.minimum(first_id + k, EX - 1)
        done = (k <= n_slots) & (bounds[1, e] <= low_pos + BLK)
        left_go = jnp.where(done, owner[0, e], -1)
        e = jnp.maximum(last_id - k, 0)
        done = (k <= n_slots) & (bounds[0, e] >= low_pos)
        go.append((left_go, jnp.where(done, owner[0, e], -1)))

    def widths(side, lo, n):
        u = uv[side, lo * 32:(lo + n) * 32, :]
        f = jnp.dot(u, qv[side * WIDE:(side + 1) * WIDE, :], preferred_element_type=f32)
        for i in range(n):
            fv[side, lo + i] = f[i * 32:(i + 1) * 32]

    def placed(o, total, slots):
        for k in slots:
            for d in range(SIDES):
                total = total + jnp.where(go[k][d] == o, 1.0, 0.0) * fv[d, (k + TOUCH - 1) % TOUCH]
        return total

    def moments_of(m, z, cc):
        a = mom[z, 0, m, :, cc].astype(f32)
        b = mom[z, 1, m, :, cc].astype(f32)
        return (
            BETA_ONE * jnp.concatenate([a[:8], b[:8]], axis=0),
            BETA_TWO * jnp.concatenate([a[8:], b[8:]], axis=0),
        )

    def normalize(scaled, g):
        first = scaled[0] + g
        second = scaled[1] + SQUARE * (g * g)
        root = second * lax.rsqrt(second) + EPSILON
        return (first * lax.rsqrt(root * root)).astype(bf16)

    def rank_side(k, m, side, n):
        row = (k + TOUCH - 1) % TOUCH * 32 + m * KR
        u = jnp.dot(r2, n, preferred_element_type=f32)
        if not isinstance(row, int):
            row = pl.multiple_of(row, KR)
        uv[side, pl.ds(row, KR), :] = (u[:KR] + u[KR:]).astype(bf16)

    def scale_moments(m, side):
        cc = half_rows(side)
        for z in range(N_Z):
            for i, v in enumerate(moments_of(m, z, cc)):
                scaled[2 * side + m, i, z * 16:z * 16 + 16, :] = v

    def seven(i, _):
        m = lax.rem(i, 2)
        side = lax.div(i, 2)
        for n, steps in (
            (0, ((2, 4),)), (1, ((2, 5),)), (2, ((2, 6), (2, 7))),
        ):
            @pl.when(i == n)
            def _():
                for place, c in steps:
                    chain(place, c)

        scale_moments(m, side)
        for k in range(1, TOUCH):
            g = parts[m, k * RANK:(k + 1) * RANK, half_rows(side)].astype(f32)
            rank_side(k, m, side, normalize((scaled[i, 0], scaled[i, 1]), g))
        return 0

    lax.fori_loop(0, 4, seven, 0)

    for d in range(SIDES):
        widths(d, 0, TOUCH - 1)

    def place_most(o, _):
        facc[o] = placed(o, jnp.zeros((2 * KR, KD), f32), range(1, TOUCH))
        return 0

    lax.fori_loop(0, GROUP, place_most, 0)

    for d in range(SIDES):
        @pl.when(places[d] == N_SEQ - 1)
        def _():
            for c in range(CHUNKS):
                chain_copy(d, c).wait_recv()

    for i in range(4):
        m = i % 2
        side = i // 2
        came = jnp.concatenate(
            [cr[side, (1 - m) * (CHUNKS // 2) + c].astype(f32) for c in range(CHUNKS // 2)], axis=0)
        g = parts[m, :RANK, side * WIDE:(side + 1) * WIDE].astype(f32) + begins[side] * (1.0 - BETA_ONE) * came
        rank_side(0, m, side, normalize((scaled[i, 0], scaled[i, 1]), g))

    for d in range(SIDES):
        widths(d, TOUCH - 1, 1)

    def feature_copy(o):
        return rcopy(
            fsend.at[o], frecv.at[me], f_ss.at[o], f_rs.at[me],
            seq=lax.div(o, N_TP), tensor=lax.rem(o, N_TP))

    def place(j, _):
        o = lax.rem(me + 1 + j, GROUP)
        fsend[o] = placed(o, facc[o], (0,)).astype(bf16)

        @pl.when(j < GROUP - 1)
        def _():
            feature_copy(o).start()

        return 0

    lax.fori_loop(0, GROUP, place, 0)
    own_feature = pltpu.make_async_copy(fsend.at[me], frecv.at[me], f_ss.at[me])
    own_feature.start()

    lax.fori_loop(6, 8, main_tile, 0)

    def out_copy(i):
        rows = pl.ds(pl.multiple_of(i * TILE, TILE), TILE)
        return pltpu.make_async_copy(outv.at[rows, :], out_hbm.at[rows, :], out_sem.at[i])

    def fix(i, _):
        rows = pl.ds(pl.multiple_of(i * TILE, TILE), TILE)
        h = lax.div(i, 2)
        sub = pl.ds(pl.multiple_of(lax.rem(i, 2) * TILE, TILE), TILE)
        corr = lax.dot_general(low[h, 0, sub, :], ab[1], NT, preferred_element_type=f32)
        outv[rows, :] = (acc[rows, :] + SCALE * corr).astype(bf16)
        out_copy(i).start()
        return 0

    lax.fori_loop(0, BLK // TILE, fix, 0)

    def arrive(j, _):
        o = lax.rem(me + j, GROUP)
        rcopy(fsend.at[o], frecv.at[o], f_ss.at[o], f_rs.at[o],
              seq=lax.div(o, N_TP), tensor=lax.rem(o, N_TP)).wait_recv()
        return 0

    lax.fori_loop(1, GROUP, arrive, 0)

    for m in range(2):
        ex1(m).wait_send()
        ex2(m).wait_send()
        ex3(m, core).wait_send()
    mx(xh).wait_send()
    for a in range(2):
        for i in range(4):
            near_copy(a, i).wait_send()
            far_copy(a, i).wait_send()

    for d in range(SIDES):
        @pl.when(places[d] < N_SEQ - 1)
        def _():
            for c in range(CHUNKS):
                chain_copy(d, c).wait_send()

    def left(j, _):
        feature_copy(lax.rem(me + j, GROUP)).wait_send()
        return 0

    lax.fori_loop(1, GROUP, left, 0)
    own_feature.wait()
    for i in range(BLK // TILE):
        out_copy(i).wait()


def finish(att_in, feat_in, att_out, feat_out, buf, fbuf, fsum, in_sem, out_sem, f_in, f_out):
    def piece(i):
        return pl.ds(i * (BLK // PIECES), BLK // PIECES)

    def load(i):
        return pltpu.make_async_copy(att_in.at[piece(i), :], buf.at[piece(i), :], in_sem.at[i])

    def store(i):
        return pltpu.make_async_copy(buf.at[piece(i), :], att_out.at[piece(i), :], out_sem.at[i])

    features = pltpu.make_async_copy(feat_in, fbuf, f_in)
    features.start()
    for i in range(PIECES):
        load(i).start()
    for i in range(PIECES):
        load(i).wait()
        store(i).start()
    features.wait()

    def add(o, total):
        return total + fbuf[o].astype(f32)

    feat = lax.fori_loop(0, GROUP, add, jnp.zeros((2 * KR, KD), f32))
    fsum[pl.ds(0, 2 * KR, stride=2), :] = feat[:, :128]
    fsum[pl.ds(1, 2 * KR, stride=2), :] = feat[:, 128:]
    result = pltpu.make_async_copy(fsum, feat_out, f_out)
    result.start()
    result.wait()
    for i in range(PIECES):
        store(i).wait()


def per_device(x, g, a, b, w, m1, m2, r, q, bounds, owner):
    any_ = pl.BlockSpec(memory_space=pl.ANY)
    dma = pltpu.SemaphoreType.DMA
    V = pltpu.VMEM
    att, arrived = pl.pallas_call(
        kernel,
        out_shape=(
            jax.ShapeDtypeStruct((BLK, COLS), bf16),
            jax.ShapeDtypeStruct((GROUP, 2 * KR, KD), bf16),
        ),
        in_specs=[any_] * 11,
        out_specs=(any_, any_),
        scratch_shapes=[
            V((2, BLK, COLS), bf16), V((BLK, WIDTH), bf16), V((COLS, WIDTH), bf16),
            V((2, COLS, RANK), bf16), V((RANK, COLS), bf16), V((COLS, KD), bf16),
            V((2, 8, COLS), f32), V((2, 8, COLS), f32), V((KR, RANK), f32),
            pltpu.SMEM((2, EX), jnp.int32), pltpu.SMEM((1, EX), jnp.int32),
            V((BLK, COLS), f32), V((BLK, COLS), bf16),
            V((2, HALF, RANK), bf16), V((2, HALF, RANK), bf16), V((2, HALF, RANK), f32),
            V((2, HALF, RANK), bf16), V((2, HALF, RANK), bf16),
            V((2, 2, HALF, RANK), bf16), V((2 * RANK, BLK), bf16),
            V((2, TOUCH * RANK, COLS), bf16),
            V((SIDES, CHUNKS, SLICE, WIDE), bf16), V((SIDES, CHUNKS, SLICE, WIDE), bf16),
            V((N_Z, 2, 2, 16, COLS), bf16), V((4, 2, RANK, WIDE), f32),
            V((SIDES, TOUCH * 32, WIDE), bf16), V((SIDES, TOUCH, 2 * KR, KD), f32),
            V((GROUP, 2 * KR, KD), f32),
            V((GROUP, 2 * KR, KD), bf16),
            dma((24,)), dma((4,)), dma((3, 2)), dma((3, 2)), dma(()), dma(()),
            dma((2, 4)), dma((2, 4)), dma((2, 4)), dma((2, 4)), dma((SIDES, CHUNKS)), dma((SIDES, CHUNKS)),
            dma((GROUP,)), dma((GROUP,)),
        ],
        compiler_params=pltpu.CompilerParams(
            collective_id=0, has_side_effects=True, vmem_limit_bytes=VLIMIT * 2**20),
        name="step",
    )(
        x.reshape(BLK, COLS), g.reshape(BLK, WIDTH), a, b, w, m1, m2, r, q,
        bounds.reshape(2, EX), owner.reshape(1, EX),
    )
    att, feat = pl.pallas_call(
        finish,
        out_shape=(
            jax.ShapeDtypeStruct((BLK, COLS), bf16),
            jax.ShapeDtypeStruct((4 * KR, KD // 2), f32),
        ),
        in_specs=[any_, any_],
        out_specs=(any_, any_),
        scratch_shapes=[
            V((BLK, COLS), bf16), V((GROUP, 2 * KR, KD), bf16), V((4 * KR, KD // 2), f32),
            dma((PIECES,)), dma((PIECES,)), dma(()), dma(()),
        ],
        compiler_params=pltpu.CompilerParams(vmem_limit_bytes=VLIMIT * 2**20),
        name="finish",
    )(att, arrived)
    return att.reshape(1, BLK, COLS), feat.reshape(1, 1, 2 * KR * KD)


def solution(mesh):
    return jax.shard_map(
        per_device,
        mesh=mesh,
        in_specs=(
            P("dp", "seq", "tensor"),
            P("dp", "seq", None),
            P("tensor", None),
            P(None, "tensor"),
            P("tensor", None),
            P(None, "dp", "tensor"),
            P(None, "dp", "tensor"),
            P(),
            P(),
            P("dp", None, None),
            P("dp", None),
        ),
        out_specs=(P("dp", "seq", "tensor"), P("dp", ("seq", "tensor"), None)),
        check_vma=False,
    )
```
